256 devices in a mesh: seq: 64 (over z, x, y_hi), tp: 4 (over y_lo, core).
Axes of the slice: x: 4, y: 4 (y_hi: 2, y_lo: 2; y = y_hi * 2 + y_lo), z: 8, core: 2. Of those that a mesh axis runs over, the one named last changes fastest.
Arguments:
- tokens: bfloat16 [36864, 3072], P('seq', 'tp'), may hold values from -6 to 6, as said below
- norm_gain: float32 [3072], replicated, may hold values from 0.1 to 1.9
- w_qkv: bfloat16 [3072, 3, 1536], P(None, None, 'tp'), may hold values from -0.649519 to 0.649519, as said below
- w_out: bfloat16 [1536, 3072], P('tp'), may hold values from -2.5 to 2.5
- sink_logit: float32 [16], P('tp'), may hold values from 4 to 8
- segment_ids: int32 [36864], P('seq'), may hold values from 0 to 30, as said below
- positions: int32 [36864], P('seq'), may hold values from 0 to 32831, as said below
- padding_mask: int32 [36864], P('seq'), may hold values from 0 to 1, as said below
Outputs:
- attn_out: bfloat16 [36864, 3072], P('seq', 'tp')
- kv_cache: bfloat16 [2, 36864, 1536], P(None, 'seq', 'tp')
The draws below stay inside these ranges and needn't reach their ends.
Inputs may be any that keep to these rules, and one draw needn't show every extreme that they name: `segment_ids`: segment 0 is one long prompt covering tokens 0 to 32831; after it come short prompts with ids rising by one: first one shorter prompt if the short region is not filled otherwise, then consecutive pairs whose two lengths sum to 256, then a last prompt of exactly 256 tokens ending at the stream's end. `positions`: the index of each token within its prompt, counted from 0 at the prompt's first token. `padding_mask`: zero only on trailing tokens of short prompts: each short prompt has at most half of its tokens padded at its end, the last prompt 1 to 128; the long prompt has none. `w_qkv`: entries within the stated bound. `tokens`: entries within the stated bound.
All inputs are finite; a program needn't handle non-finite values.
Results may differ from the reference program's by a relative error of at most 0.015.
Values may be sent and summed in bfloat16 or wider, within the bound.
A program may use at most 128 MiB of HBM per device.

```python
import jax
import jax.numpy as jnp
from jax import lax

D = 3072
HEADS = 16
HD = 96
TOK_DEV = 576
WINDOW = 4096
SINKS = 4
SHORT_DEVS = 7
SHORT_MOST = 256
STREAM = 36864
LONG = 32832
N_SEQ = 64
N_TP = 4


def draw_tokens(key, part):
    shape = (STREAM, D)
    direction = jax.random.truncated_normal(jax.random.fold_in(key, 21), -3.0, 3.0, (D,), jnp.float32)
    rough_part = jax.random.truncated_normal(jax.random.fold_in(key, 22), -5.0, 5.0, shape, jnp.float32)
    full = rough_part + 0.08 * direction[None, :]
    return full.astype(jnp.bfloat16)


def draw_w_qkv(key, part):
    shape = (D, 3, HEADS * HD)
    base = jax.random.truncated_normal(jax.random.fold_in(key, 11), -6.0, 6.0, shape, jnp.float32)
    full = base * D ** (-0.5)
    return full.astype(jnp.bfloat16)


def stream_layout(key):
    base = jax.random.fold_in(key, 7)
    first, second, third = jax.random.split(base, 3)
    region = SHORT_DEVS * TOK_DEV - SHORT_MOST
    pairs = region // SHORT_MOST
    remain = region % SHORT_MOST
    pieces = []
    if remain > 0:
        pieces.append(jnp.full((1,), remain, jnp.int32))
    if pairs > 0:
        lead = jax.random.randint(first, (pairs,), 1, SHORT_MOST, dtype=jnp.int32)
        pieces.append(jnp.stack([lead, SHORT_MOST - lead], axis=1).reshape(2 * pairs).astype(jnp.int32))
    pieces.append(jnp.full((1,), SHORT_MOST, jnp.int32))
    lengths = jnp.concatenate(pieces).astype(jnp.int32)
    count = lengths.shape[0]
    pads = jax.random.randint(second, (count,), 0, lengths // 2 + 1, dtype=jnp.int32)
    last_pad = jax.random.randint(third, (), 1, SHORT_MOST // 2 + 1, dtype=jnp.int32)
    pads = pads.at[count - 1].set(last_pad)
    bounds = LONG + jnp.cumsum(lengths).astype(jnp.int32)
    places = jnp.arange(STREAM, dtype=jnp.int32)
    passed = jnp.searchsorted(bounds, places, side='right').astype(jnp.int32)
    segment = jnp.where(places < LONG, 0, 1 + passed).astype(jnp.int32)
    starts = jnp.concatenate([jnp.array([0, LONG], jnp.int32), bounds])
    begin = starts[segment]
    position = (places - begin).astype(jnp.int32)
    index = jnp.clip(passed, 0, count - 1).astype(jnp.int32)
    ends = bounds[index]
    cut = pads[index]
    valid = jnp.where(places < LONG, 1, (places < ends - cut).astype(jnp.int32)).astype(jnp.int32)
    return (segment, position, valid)


def draw_segment_ids(key, part):
    return stream_layout(key)[0]


def draw_positions(key, part):
    return stream_layout(key)[1]


def draw_padding_mask(key, part):
    return stream_layout(key)[2]


def block_levels(key, dims, cuts, smallest, largest):
    level, own = 1.0, jax.random.fold_in(key, 6)
    for dim, parts in cuts:
        steps = jnp.exp(jax.random.uniform(jax.random.fold_in(own, dim), (parts,), jnp.float32, smallest / len(cuts), largest / len(cuts)))
        level = level * jnp.repeat(steps, dims[dim] // parts).reshape([-1 if axis == dim else 1 for axis in range(len(dims))])
    return level


def scatter_about(stream_key, extent, scale, most, cuts=(), kind=jnp.bfloat16):
    entries = jax.random.normal(stream_key, extent, jnp.float32) * scale
    if len(cuts) > 0:
        entries = block_levels(stream_key, extent, cuts, -0.22, 0.18) * entries
    return jnp.clip(entries, min=-most, max=most).astype(kind)


def setup_inputs(seed: int = 0) -> dict:
    key_list = jax.random.split(jax.random.key(seed), 9)
    return {
        "tokens": draw_tokens(jax.random.fold_in(key_list[8], 71), 0),
        "norm_gain": jnp.clip(1.0 + 0.18 * jax.random.normal(key_list[1], (D,), jnp.float32), 0.1, 1.9),
        "w_qkv": draw_w_qkv(jax.random.fold_in(key_list[8], 71), 0),
        "w_out": scatter_about(key_list[3], (HEADS * HD, D), (HD // 16) ** -0.5, 2.5, ((0, 4),)),
        "sink_logit": jnp.clip(4.0 + 4.0 * jax.random.uniform(key_list[4], (HEADS,), jnp.float32) ** block_levels(key_list[4], (HEADS,), ((0, 4),), -0.2, 0.2), 4.0, 8.0),
        "segment_ids": draw_segment_ids(jax.random.fold_in(key_list[8], 71), 0),
        "positions": draw_positions(jax.random.fold_in(key_list[8], 71), 0),
        "padding_mask": draw_padding_mask(jax.random.fold_in(key_list[8], 71), 0),
    }


EPS = 1e-05
THETA = 10000.0

def rope(x, pos):
    half = x.shape[-1] // 2
    freq = THETA ** (-(jnp.arange(half, dtype=jnp.float32) * 2.0 / x.shape[-1]))
    angle = pos.astype(jnp.float32)[:, None] * freq[None, :]
    cosine = jnp.cos(angle)[:, None, :]
    sine = jnp.sin(angle)[:, None, :]
    first = x[..., :half]
    second = x[..., half:]
    return jnp.concatenate([first * cosine - second * sine, second * cosine + first * sine], axis=-1)

def reference(tokens, norm_gain, w_qkv, w_out, sink_logit, segment_ids, positions, padding_mask):
    total_rows = tokens.shape[0]
    xf = tokens.astype(jnp.float32)
    meansq = lax.optimization_barrier(jnp.mean(xf * xf, axis=-1, keepdims=True))
    normed = (xf * lax.rsqrt(meansq + EPS) * norm_gain).astype(jnp.bfloat16)
    qkv = jnp.dot(normed, w_qkv.reshape(D, 3 * HEADS * HD), preferred_element_type=jnp.float32)
    qkv = qkv.reshape(total_rows, 3, HEADS, HD)
    query = rope(qkv[:, 0], positions).astype(jnp.bfloat16)
    key = rope(qkv[:, 1], positions).astype(jnp.bfloat16)
    value = qkv[:, 2].astype(jnp.bfloat16)
    keep = padding_mask[:, None, None].astype(jnp.bfloat16)
    kv_cache = jnp.stack([(key * keep).reshape(total_rows, HEADS * HD), (value * keep).reshape(total_rows, HEADS * HD)])
    reach = (WINDOW - 1 + TOK_DEV - 1) // TOK_DEV
    front = reach * TOK_DEV
    key_pad = jnp.concatenate([jnp.zeros((front, HEADS, HD), jnp.bfloat16), key])
    value_pad = jnp.concatenate([jnp.zeros((front, HEADS, HD), jnp.bfloat16), value])
    seg_pad = jnp.concatenate([jnp.full((front,), -1, jnp.int32), segment_ids.astype(jnp.int32)])
    pos_pad = jnp.concatenate([jnp.zeros((front,), jnp.int32), positions.astype(jnp.int32)])
    valid_pad = jnp.concatenate([jnp.zeros((front,), jnp.int32), padding_mask.astype(jnp.int32)])
    scale = HD ** (-0.5)
    span = (reach + 1) * TOK_DEV

    def block(index):
        qstart = (index * TOK_DEV).astype(jnp.int32)
        qrows = qstart + jnp.arange(TOK_DEV, dtype=jnp.int32)
        qblk = lax.dynamic_slice_in_dim(query, qstart, TOK_DEV, 0).astype(jnp.float32)
        segq = lax.dynamic_slice_in_dim(segment_ids, qstart, TOK_DEV, 0)
        posq = lax.dynamic_slice_in_dim(positions, qstart, TOK_DEV, 0)
        kblk = lax.dynamic_slice_in_dim(key_pad, qstart, span, 0).astype(jnp.float32)
        vblk = lax.dynamic_slice_in_dim(value_pad, qstart, span, 0).astype(jnp.float32)
        segk = lax.dynamic_slice_in_dim(seg_pad, qstart, span, 0)
        posk = lax.dynamic_slice_in_dim(pos_pad, qstart, span, 0)
        validk = lax.dynamic_slice_in_dim(valid_pad, qstart, span, 0)
        krows = qstart - front + jnp.arange(span, dtype=jnp.int32)
        bias = jnp.where(posk[None, None, :] < SINKS, sink_logit[:, None, None], 0.0)
        scores_w = jnp.einsum('qhd,khd->hqk', qblk, kblk) * scale + bias
        seen_w = (krows[None, :] >= 0) & (krows[None, :] <= qrows[:, None]) & (qrows[:, None] - krows[None, :] < WINDOW)
        seen_w = seen_w & (segk[None, :] == segq[:, None]) & ((validk[None, :] == 1) | (krows[None, :] == qrows[:, None]))
        starts = qrows - posq
        sink_rows = starts[:, None] + jnp.arange(SINKS, dtype=jnp.int32)[None, :]
        inside = (sink_rows >= 0) & (sink_rows < total_rows)
        clipped = jnp.clip(sink_rows, 0, total_rows - 1).astype(jnp.int32)
        ksink = key[clipped].astype(jnp.float32)
        vsink = value[clipped].astype(jnp.float32)
        seen_s = inside & (sink_rows <= qrows[:, None] - WINDOW) & (segment_ids[clipped] == segq[:, None]) & (padding_mask[clipped] == 1)
        scores_s = jnp.einsum('qhd,qshd->hqs', qblk, ksink) * scale + sink_logit[:, None, None]
        top_w = lax.optimization_barrier(jnp.max(jnp.where(seen_w[None], scores_w, -1e+30), axis=-1))
        top_s = lax.optimization_barrier(jnp.max(jnp.where(seen_s[None], scores_s, -1e+30), axis=-1))
        top = jnp.maximum(top_w, top_s)
        weight_w = jnp.where(seen_w[None], jnp.exp(scores_w - top[..., None]), 0.0)
        weight_s = jnp.where(seen_s[None], jnp.exp(scores_s - top[..., None]), 0.0)
        total = lax.optimization_barrier(jnp.sum(weight_w, axis=-1)) + lax.optimization_barrier(jnp.sum(weight_s, axis=-1))
        mixed = jnp.einsum('hqk,khd->qhd', weight_w.astype(jnp.bfloat16).astype(jnp.float32), vblk)
        mixed = mixed + jnp.einsum('hqs,qshd->qhd', weight_s.astype(jnp.bfloat16).astype(jnp.float32), vsink)
        mixed = mixed / total.transpose()[:, :, None]
        return mixed.astype(jnp.bfloat16).reshape(TOK_DEV, HEADS * HD)
    mixed_all = lax.map(block, jnp.arange(N_SEQ, dtype=jnp.int32)).reshape(total_rows, HEADS * HD)
    group = HEADS * HD // N_TP
    summed = jnp.zeros((total_rows, D), jnp.float32)
    for part_index in range(N_TP):
        partial_value = jnp.dot(mixed_all[:, part_index * group:(part_index + 1) * group], w_out[part_index * group:(part_index + 1) * group], preferred_element_type=jnp.float32)
        partial_value = lax.optimization_barrier(partial_value.astype(jnp.bfloat16))
        summed = summed + partial_value.astype(jnp.float32)
    return (summed.astype(jnp.bfloat16), kv_cache)
```

```python
import functools
import math

import jax
import jax.numpy as jnp
from jax import lax
from jax.experimental import pallas as pl
from jax.experimental.pallas import tpu as pltpu
from jax.sharding import PartitionSpec as P

WINDOW = 4096
SINKS = 4
EPS = 1e-05
THETA = 10000.0
LONG = 32832

ROWS = 576
MODEL = 3072
PART = 768
WIDTH = 384
HD = 96
PAD = 128
GROUP = 2304
TILE = 256
CHUNK = 144
STEPS = 4
PREV1 = GROUP
OWN = 2 * GROUP
SINK_AT = 3 * GROUP
SPAN = 3 * GROUP + 16
FAR = 512
NEG = -1e30
MESH = pl.DeviceIdType.MESH
ANY = pl.BlockSpec(memory_space=pl.ANY)
VM = pl.BlockSpec(memory_space=pltpu.VMEM)


def place():
    seq = lax.axis_index("seq")
    tp = lax.axis_index("tp")
    return seq, tp, tp // 2, tp % 2


def remote(src, dst, send, recv, seq, tp):
    return pltpu.make_async_remote_copy(
        src_ref=src,
        dst_ref=dst,
        send_sem=send,
        recv_sem=recv,
        device_id=(seq, tp),
        device_id_type=MESH,
    )


def greet(seq, tp):
    pl.semaphore_signal(
        pltpu.get_barrier_semaphore(), inc=1, device_id=(seq, tp), device_id_type=MESH
    )


def lanes(rows):
    return lax.broadcasted_iota(jnp.int32, (rows, PAD), 1)


def project_kernel(
    x_ref, gain_ref, w_ref, cos_ref, sin_ref, kmark_ref, qmark_ref, sink_ref,
    q_ref, kv_ref, cache_ref,
    held, weights, acc, square, wsem, xsem, send, recv,
):
    seq, tp, yl, core = place()
    mate = yl * 2 + 1 - core
    cross = (1 - yl) * 2 + core
    far = (1 - yl) * 2 + 1 - core
    order = (tp, mate, cross, far)
    own = pltpu.make_async_copy(x_ref, held.at[0], xsem)
    own.start()

    def weight_copy(k):
        start = pl.multiple_of(order[k] * PART, PART)
        return pltpu.make_async_copy(
            w_ref.at[:, pl.ds(start, PART), :], weights.at[k], wsem.at[k]
        )

    for k in range(4):
        weight_copy(k).start()
    greet(seq, mate)
    greet(seq, cross)
    pl.semaphore_wait(pltpu.get_barrier_semaphore(), 2)

    def part(c):
        return pl.ds(c * CHUNK, CHUNK)

    to_cross = [
        remote(x_ref.at[part(c)], held.at[2, part(c)], send.at[c], recv.at[c], seq, cross)
        for c in range(STEPS)
    ]
    for copy in to_cross:
        copy.start()
    to_mate = remote(x_ref, held.at[1], send.at[8], recv.at[8], seq, mate)
    to_mate.start()

    def block(k):
        @pl.loop(0, STEPS)
        def _(c):
            rows = pl.ds(pl.multiple_of(c * CHUNK, CHUNK), CHUNK)
            x = held[k, rows, :].astype(jnp.float32)
            sums = jnp.sum(x * x, axis=-1, keepdims=True)
            y = (x * gain_ref[order[k]]).astype(jnp.bfloat16)
            if k == 0:
                square[rows, :] = sums
            else:
                square[rows, :] += sums
            for j in range(3):
                cols = pl.ds(j * WIDTH, WIDTH)
                term = jnp.dot(y, weights[k, j], preferred_element_type=jnp.float32)
                if k == 0:
                    acc[rows, cols] = term
                else:
                    acc[rows, cols] += term

    own.wait()
    weight_copy(0).wait()
    block(0)
    to_mate.wait_recv()
    weight_copy(1).wait()
    block(1)
    onward = []
    for c in range(STEPS):
        to_cross[c].wait_recv()
        copy = remote(
            held.at[2, part(c)], held.at[3, part(c)], send.at[4 + c], recv.at[4 + c], seq, mate
        )
        copy.start()
        onward.append(copy)
    weight_copy(2).wait()
    block(2)
    for c in range(STEPS):
        onward[c].wait_recv()
    weight_copy(3).wait()
    block(3)

    @pl.loop(0, STEPS)
    def _(c):
        rows = pl.ds(pl.multiple_of(c * CHUNK, CHUNK), CHUNK)
        lane = lanes(CHUNK)
        factor = lax.rsqrt(square[rows, :] / MODEL + EPS)
        kmark = kmark_ref[rows, :]
        qmark = qmark_ref[rows, :]
        valid = 1.0 - kmark[:, 100:101]
        cosine = cos_ref[rows, :]
        sine = sin_ref[rows, :]

        def heads(j):
            b = [acc[rows, pl.ds(j * WIDTH + n * PAD, PAD)] * factor for n in range(3)]
            return b, [
                b[0],
                jnp.where(lane < 32, pltpu.roll(b[0], 32, 1), pltpu.roll(b[1], 32, 1)),
                jnp.where(lane < 64, pltpu.roll(b[1], 64, 1), pltpu.roll(b[2], 64, 1)),
                pltpu.roll(b[2], 96, 1),
            ]

        def turn(u):
            other = jnp.where(lane < 48, pltpu.roll(u, 80, 1), pltpu.roll(u, 48, 1))
            return jnp.where(lane < HD, u * cosine + other * sine, 0.0)

        for h, u in enumerate(heads(0)[1]):
            full = turn(u) * (HD ** -0.5 / math.log(2.0)) + qmark + sink_ref[h]
            q_ref[h, rows, :] = full.astype(jnp.bfloat16)
        keys = []
        for h, u in enumerate(heads(1)[1]):
            k = turn(u)
            keys.append(k)
            kv_ref[h, rows, 0:PAD] = (k + kmark).astype(jnp.bfloat16)
        k1, k2, k3 = (pltpu.roll(keys[1], 96, 1), pltpu.roll(keys[2], 64, 1), pltpu.roll(keys[3], 32, 1))
        joined = (
            jnp.where(lane < 96, keys[0], k1),
            jnp.where(lane < 64, k1, k2),
            jnp.where(lane < 32, k2, k3),
        )
        plain, values = heads(2)
        for n in range(3):
            cols = pl.ds(n * PAD, PAD)
            cache_ref[0, rows, cols] = (joined[n] * valid).astype(jnp.bfloat16)
            cache_ref[1, rows, cols] = (plain[n] * valid).astype(jnp.bfloat16)
        for h, u in enumerate(values):
            v = jnp.where(lane < HD, u, jnp.where(lane == HD, 1.0, 0.0))
            kv_ref[h, rows, PAD:] = v.astype(jnp.bfloat16)

    for c in range(STEPS):
        to_cross[c].wait_send()
        onward[c].wait_send()
    to_mate.wait_send()


def exchange_kernel(
    q_ref, kv_ref, wo_ref, qo_ref, kvo_ref, wg_ref,
    a_send, a_recv, x_send, z_send, one_recv, two_recv, s_send, s_recv, w_send, w_recv,
):
    seq, tp, yl, core = place()
    group = seq // 4
    m = seq % 4
    z = seq // 8
    xp = group % 2
    xb = m // 2
    hy = m % 2
    hx = xb + xp - 2 * xp * xb
    mate = yl * 2 + 1 - core
    cross = (1 - yl) * 2 + core
    far = (1 - yl) * 2 + 1 - core
    flipped = seq + 1 - 2 * hy
    beside = 4 * (group + 1 - 2 * xp) + (1 - xb) * 2 + hy
    root = hx * 2 + hy

    def holder(g):
        odd = g % 2
        return 4 * g + (hx + odd - 2 * odd * hx) * 2 + hy

    for d in range(4):
        greet(4 * group + d, cross)
    greet(seq, mate)
    greet(flipped, far)
    greet(beside, tp)

    @pl.when(z > 0)
    def _():
        greet(seq - 8, tp)

    @pl.when(z < 7)
    def _():
        greet(seq + 8, tp)

    @pl.when(group == 0)
    def _():
        @pl.loop(1, 16)
        def _(g):
            greet(holder(g), tp)

    @pl.when(group > 0)
    def _():
        greet(root, tp)

    count = 7 + jnp.where(z > 0, 1, 0) + jnp.where(z < 7, 1, 0) + jnp.where(group == 0, 15, 1)
    pl.semaphore_wait(pltpu.get_barrier_semaphore(), count)

    def own_rows(s):
        return pl.ds(pl.multiple_of(OWN + s * ROWS, 64), ROWS)

    def q_rows(s):
        return pl.ds(pl.multiple_of(s * ROWS, 64), ROWS)

    sends = []
    for d in range(4):
        b = d // 2
        h = (b + xp - 2 * xp * b) * 2 + d % 2
        copy = remote(
            kv_ref.at[h], kvo_ref.at[own_rows(m)], a_send.at[d, 0], a_recv.at[m, 0], 4 * group + d, cross
        )
        copy.start()
        sends.append(copy)
    for d in range(4):
        b = d // 2
        h = (b + xp - 2 * xp * b) * 2 + d % 2
        copy = remote(
            q_ref.at[h], qo_ref.at[q_rows(m)], a_send.at[d, 1], a_recv.at[m, 1], 4 * group + d, cross
        )
        copy.start()
        sends.append(copy)

    def columns(t):
        return pl.ds(pl.multiple_of(t * PART, PART), PART)

    for n, (s2, t2) in enumerate(((seq, mate), (seq, cross), (flipped, far))):
        copy = remote(wo_ref.at[:, columns(t2)], wg_ref.at[n], w_send.at[n], w_recv.at[n], s2, t2)
        copy.start()
        sends.append(copy)

    def arrived(ref, sem):
        pltpu.make_async_copy(ref, ref, sem).wait()

    def tail(s):
        return pl.ds(s * ROWS + (FAR if s == 0 else 0), 64 if s == 0 else ROWS)

    def whole(s):
        return pl.ds(s * ROWS, ROWS)

    def after(s):
        return pl.ds(PREV1 + s * ROWS, ROWS)

    def mine(s):
        return pl.ds(OWN + s * ROWS, ROWS)

    def mine_tail(s):
        return pl.ds(OWN + s * ROWS + (FAR if s == 0 else 0), 64 if s == 0 else ROWS)

    def across(s):
        return remote(kvo_ref.at[mine(s)], kvo_ref.at[after(s)], x_send.at[s], one_recv.at[s], beside, tp)

    def passed(s):
        return remote(kvo_ref.at[whole(s)], kvo_ref.at[after(s)], x_send.at[s], one_recv.at[s], beside, tp)

    def ahead(s):
        return remote(kvo_ref.at[mine(s)], kvo_ref.at[whole(s)], z_send.at[s], two_recv.at[s], seq + 8, tp)

    def ahead_tail(s):
        return remote(
            kvo_ref.at[mine_tail(s)], kvo_ref.at[tail(s)], z_send.at[s], two_recv.at[s], seq + 8, tp
        )

    def sink_copy(g):
        return remote(
            kvo_ref.at[pl.ds(OWN, 16)], kvo_ref.at[pl.ds(SINK_AT, 16)], s_send.at[g], s_recv, holder(g), tp
        )

    for s in range(4):
        arrived(kvo_ref.at[mine(s)], a_recv.at[s, 0])

        @pl.when(xp == 0)
        def _():
            across(s).start()

        if s == 0:
            @pl.when(group == 0)
            def _():
                @pl.loop(1, 16)
                def _(g):
                    sink_copy(g).start()

        @pl.when((xp == 0) & (z < 7))
        def _():
            ahead_tail(s).start()

        @pl.when((xp == 1) & (z < 7))
        def _():
            ahead(s).start()

    @pl.when((xp == 1) & (z > 0))
    def _():
        for s in range(4):
            arrived(kvo_ref.at[whole(s)], two_recv.at[s])
            passed(s).start()

    @pl.when((xp == 0) & (z > 0))
    def _():
        for s in range(4):
            arrived(kvo_ref.at[tail(s)], two_recv.at[s])

    @pl.when((xp == 1) | (z > 0))
    def _():
        for s in range(4):
            arrived(kvo_ref.at[after(s)], one_recv.at[s])

    @pl.when(group > 0)
    def _():
        arrived(kvo_ref.at[pl.ds(SINK_AT, 16)], s_recv)

    for s in range(4):
        arrived(qo_ref.at[whole(s)], a_recv.at[s, 1])
    for n in range(3):
        arrived(wg_ref.at[n], w_recv.at[n])
    for copy in sends:
        copy.wait_send()

    @pl.when(xp == 0)
    def _():
        for s in range(4):
            across(s).wait_send()

    @pl.when((xp == 1) & (z > 0))
    def _():
        for s in range(4):
            passed(s).wait_send()

    @pl.when((xp == 0) & (z < 7))
    def _():
        for s in range(4):
            ahead_tail(s).wait_send()

    @pl.when((xp == 1) & (z < 7))
    def _():
        for s in range(4):
            ahead(s).wait_send()

    @pl.when(group == 0)
    def _():
        @pl.loop(1, 16)
        def _(g):
            sink_copy(g).wait_send()


def dot_t(a, b):
    return lax.dot_general(a, b, (((1,), (1,)), ((), ())), preferred_element_type=jnp.float32)


def attend_kernel(q_ref, kvh_ref, o_ref, kv, scores, sem):
    seq = lax.axis_index("seq")
    group = seq // 4

    def load(start, size, n):
        return pltpu.make_async_copy(
            kvh_ref.at[pl.ds(start, size)], kv.at[pl.ds(start, size)], sem.at[n]
        )

    def blank(start, size):
        mark = lax.broadcasted_iota(jnp.int32, (16, 2 * PAD), 1)
        row = jnp.where(mark == 102, 1.0, 0.0).astype(jnp.bfloat16)

        @pl.loop(0, size // 16)
        def _(n):
            kv[pl.ds(pl.multiple_of(start + n * 16, 16), 16), :] = row

    pieces = ((OWN, GROUP, 0), (PREV1, GROUP, 1), (FAR, GROUP - FAR, 2), (SINK_AT, 16, 1))
    for n, (start, size, least) in enumerate(pieces):
        @pl.when(group >= least)
        def _():
            load(start, size, n).start()

        @pl.when(group < least)
        def _():
            blank(start, size)

    for n, (start, size, least) in enumerate(pieces):
        @pl.when(group >= least)
        def _():
            load(start, size, n).wait()

    def key(start, size):
        return kv[pl.ds(pl.multiple_of(start, TILE), size), 0:PAD]

    def val(start, size):
        return kv[pl.ds(pl.multiple_of(start, TILE), size), PAD:]

    down = lax.broadcasted_iota(jnp.int32, (TILE, TILE), 0)
    right = lax.broadcasted_iota(jnp.int32, (TILE, TILE), 1)
    lower = right <= down
    sink_k = kv[pl.ds(SINK_AT, 16), 0:PAD]
    sink_v = kv[pl.ds(SINK_AT, 16), PAD:]
    small_down = lax.broadcasted_iota(jnp.int32, (TILE, 16), 0)
    small_right = lax.broadcasted_iota(jnp.int32, (TILE, 16), 1)

    def finish(rows, acc):
        lane = lanes(TILE)
        out = acc * (1.0 / acc[:, HD:HD + 1])
        o_ref[rows, :] = jnp.where(lane < HD, out, 0.0).astype(jnp.bfloat16)

    def long_tile(i, rows, first):
        q = q_ref[rows, :]
        near = OWN + i * TILE
        outer = FAR + i * TILE
        s = jnp.where(lower, dot_t(q, key(near, TILE)), dot_t(q, key(outer, TILE)))
        scores[:, 0:TILE] = s
        top = jnp.maximum(s[:, :PAD], s[:, PAD:])
        distance = first + small_down - small_right
        seen = (small_right < SINKS) & (distance >= WINDOW)
        sink_s = jnp.where(seen, dot_t(q, sink_k), NEG)
        for c in range(5):
            s = dot_t(q, key(outer + TILE + c * 768, 768))
            scores[:, pl.ds(TILE + c * 768, 768)] = s
            for n in range(6):
                top = jnp.maximum(top, s[:, n * PAD:(n + 1) * PAD])
        peak = jnp.maximum(
            jnp.max(top, axis=-1, keepdims=True), jnp.max(sink_s, axis=-1, keepdims=True)
        )
        w = jnp.where(seen, jnp.exp2(sink_s - peak), 0.0).astype(jnp.bfloat16)
        acc = jnp.dot(w, sink_v, preferred_element_type=jnp.float32)
        w = jnp.exp2(scores[:, 0:TILE] - peak)
        acc += jnp.dot(
            jnp.where(lower, w, 0.0).astype(jnp.bfloat16), val(near, TILE), preferred_element_type=jnp.float32
        )
        acc += jnp.dot(
            jnp.where(lower, 0.0, w).astype(jnp.bfloat16), val(outer, TILE), preferred_element_type=jnp.float32
        )
        for c in range(5):
            w = jnp.exp2(scores[:, pl.ds(TILE + c * 768, 768)] - peak).astype(jnp.bfloat16)
            acc += jnp.dot(w, val(outer + TILE + c * 768, 768), preferred_element_type=jnp.float32)
        finish(rows, acc)

    def mixed_tile(i, rows, first):
        q = q_ref[rows, :]
        lane = lanes(TILE)
        qf = q.astype(jnp.float32)
        mine = qf[:, 101:102]
        pick = jnp.where(lane == 96, -1.0, jnp.where(lane == 97, mine, 0.0)).astype(jnp.bfloat16)
        lost = jnp.where(lane == 100, 1.0, 0.0).astype(jnp.bfloat16)
        distance = first + small_down - small_right
        seen = (small_right < SINKS) & (distance >= WINDOW) & (dot_t(pick, sink_k) == 0.0)
        sink_s = jnp.where(seen, dot_t(q, sink_k), NEG)
        peak = jnp.max(sink_s, axis=-1, keepdims=True)
        w = jnp.where(seen, jnp.exp2(sink_s - peak), 0.0).astype(jnp.bfloat16)
        acc = jnp.dot(w, sink_v, preferred_element_type=jnp.float32)
        low = jnp.where(first >= LONG, 15, 0)

        def step(n, carry):
            peak, acc = carry
            start = FAR + i * TILE + n * TILE
            k = key(start, TILE)
            gap = (16 - n) * TILE + down - right
            bad = dot_t(lost, k)
            seen = (gap >= 0) & (gap < WINDOW) & (dot_t(pick, k) == 0.0) & ((bad < 0.5) | (gap == 0))
            s = jnp.where(seen, dot_t(q, k), NEG)
            now = jnp.maximum(peak, jnp.max(s, axis=-1, keepdims=True))
            w = jnp.where(seen, jnp.exp2(s - now), 0.0).astype(jnp.bfloat16)
            acc = acc * jnp.exp2(peak - now) + jnp.dot(w, val(start, TILE), preferred_element_type=jnp.float32)
            return now, acc

        peak, acc = lax.fori_loop(low, 17, step, (peak, acc))
        finish(rows, acc)

    @pl.loop(0, GROUP // TILE)
    def _(i):
        rows = pl.ds(pl.multiple_of(i * TILE, TILE), TILE)
        first = group * GROUP + i * TILE

        @pl.when(first + TILE <= LONG)
        def _():
            long_tile(i, rows, first)

        @pl.when(first + TILE > LONG)
        def _():
            mixed_tile(i, rows, first)


def gather_kernel(o_ref, mg_ref, send, recv, lsem):
    seq, tp, yl, core = place()
    group = seq // 4
    m = seq % 4
    xp = group % 2
    mate = yl * 2 + 1 - core
    partner = core + 1 - 2 * core

    def head(member, low, who):
        b = member // 2
        return 4 * ((1 - low) * 2 + who) + (b + xp - 2 * xp * b) * 2 + member % 2

    mine = head(m, yl, core)
    greet(seq, mate)
    for d in range(4):
        for low in range(2):
            @pl.when((m != d) | (yl != low))
            def _():
                greet(4 * group + d, low * 2 + core)
    pl.semaphore_wait(pltpu.get_barrier_semaphore(), 8)

    def out(d, low):
        return remote(
            o_ref.at[pl.ds(d * ROWS, ROWS)], mg_ref.at[mine],
            send.at[d * 2 + low], recv.at[mine], 4 * group + d, low * 2 + core,
        )

    def local(d):
        return pltpu.make_async_copy(o_ref.at[pl.ds(d * ROWS, ROWS)], mg_ref.at[mine], lsem)

    def onward(d, low):
        g = head(d, low, core)
        return remote(mg_ref.at[g], mg_ref.at[g], send.at[8 + d * 2 + low], recv.at[g], seq, mate)

    def arrived(g):
        pltpu.make_async_copy(mg_ref.at[g], mg_ref.at[g], recv.at[g]).wait()

    for d in range(4):
        for low in range(2):
            @pl.when((m != d) | (yl != low))
            def _():
                out(d, low).start()

            @pl.when((m == d) & (yl == low))
            def _():
                local(d).start()

    for d in range(4):
        for low in range(2):
            @pl.when((m != d) | (yl != low))
            def _():
                arrived(head(d, low, core))

            @pl.when((m == d) & (yl == low))
            def _():
                local(d).wait()

            onward(d, low).start()
    for d in range(4):
        for low in range(2):
            arrived(head(d, low, partner))
    for d in range(4):
        for low in range(2):
            @pl.when((m != d) | (yl != low))
            def _():
                out(d, low).wait_send()

            onward(d, low).wait_send()


def output_kernel(mg_ref, wo_ref, wg_ref, y_ref, own, padded, sem):
    seq, tp, yl, core = place()
    order = (tp, yl * 2 + 1 - core, (1 - yl) * 2 + core, (1 - yl) * 2 + 1 - core)
    copy = pltpu.make_async_copy(wo_ref.at[:, pl.ds(pl.multiple_of(tp * PART, PART), PART)], own, sem)
    copy.start()
    for n in range(16):
        padded[pl.ds(n * PAD + HD, PAD - HD), :] = jnp.zeros((PAD - HD, PART), jnp.bfloat16)
    for n in range(12):
        padded[pl.ds((n + 4) * PAD, HD), :] = wg_ref[n // 4, pl.ds(n % 4 * HD, HD), :]
    copy.wait()
    for n in range(4):
        padded[pl.ds(n * PAD, HD), :] = own[pl.ds(n * HD, HD), :]

    @pl.loop(0, STEPS)
    def _(c):
        rows = pl.ds(pl.multiple_of(c * CHUNK, CHUNK), CHUNK)
        left = jnp.concatenate(
            [mg_ref[4 * order[n // 4] + n % 4, rows, :] for n in range(16)], axis=1
        )
        y_ref[rows, :] = jnp.dot(left, padded[...], preferred_element_type=jnp.float32).astype(jnp.bfloat16)


def shards(tokens, norm_gain, w_qkv, w_out, sink_logit, segment_ids, positions, padding_mask):
    bf16, f32 = jnp.bfloat16, jnp.float32
    spot = jnp.arange(PAD, dtype=jnp.int32)
    freq = THETA ** (-((spot % 48).astype(f32) * 2.0 / HD))
    angle = positions.astype(f32)[:, None] * freq[None, :]
    cosine = jnp.cos(angle)
    sine = jnp.where(spot[None, :] < 48, -jnp.sin(angle), jnp.sin(angle))
    seg = segment_ids.astype(f32)[:, None]
    sinkish = (positions < SINKS).astype(f32)[:, None]
    lost = 1.0 - padding_mask.astype(f32)[:, None]
    kmark = jnp.where(spot == 96, seg, 0.0) + jnp.where(spot == 97, 1.0, 0.0)
    kmark = kmark + jnp.where((spot == 98) | (spot == 99), sinkish, 0.0) + jnp.where(spot == 100, lost, 0.0)
    qmark = jnp.where(spot == 101, seg, 0.0) + jnp.where(spot == 102, NEG, 0.0)
    logit = sink_logit * (1.0 / math.log(2.0))
    high = lax.reduce_precision(logit, 8, 7)
    low = logit - high
    sink = jnp.where(spot == 98, high[:, None], 0.0) + jnp.where(spot == 99, low[:, None], 0.0)
    sink = sink.reshape(4, 1, PAD)

    dma = pltpu.SemaphoreType.DMA
    q, kv, cache = pl.pallas_call(
        project_kernel,
        out_shape=(
            jax.ShapeDtypeStruct((4, ROWS, PAD), bf16),
            jax.ShapeDtypeStruct((4, ROWS, 2 * PAD), bf16),
            jax.ShapeDtypeStruct((2, ROWS, WIDTH), bf16),
        ),
        in_specs=[ANY, VM, ANY, VM, VM, VM, VM, VM],
        out_specs=(VM, VM, VM),
        scratch_shapes=[
            pltpu.VMEM((4, ROWS, PART), bf16),
            pltpu.VMEM((4, 3, PART, WIDTH), bf16),
            pltpu.VMEM((ROWS, 3 * WIDTH), f32),
            pltpu.VMEM((ROWS, 1), f32),
            dma((4,)),
            dma,
            dma((9,)),
            dma((9,)),
        ],
        compiler_params=pltpu.CompilerParams(collective_id=0, has_side_effects=True),
        name="project",
    )(
        tokens, norm_gain.reshape(4, 1, PART), jnp.transpose(w_qkv, (1, 0, 2)),
        cosine, sine, kmark, qmark, sink,
    )
    qo, kvo, wg = pl.pallas_call(
        exchange_kernel,
        out_shape=(
            jax.ShapeDtypeStruct((GROUP, PAD), bf16),
            jax.ShapeDtypeStruct((SPAN, 2 * PAD), bf16),
            jax.ShapeDtypeStruct((3, WIDTH, PART), bf16),
        ),
        in_specs=[ANY, ANY, ANY],
        out_specs=(ANY, ANY, ANY),
        scratch_shapes=[
            dma((4, 2)), dma((4, 2)), dma((4,)), dma((4,)), dma((4,)), dma((4,)),
            dma((16,)), dma, dma((3,)), dma((3,)),
        ],
        compiler_params=pltpu.CompilerParams(collective_id=1, has_side_effects=True),
        name="exchange",
    )(q, kv, w_out)
    mixed = pl.pallas_call(
        attend_kernel,
        out_shape=jax.ShapeDtypeStruct((GROUP, PAD), bf16),
        in_specs=[VM, ANY],
        out_specs=VM,
        scratch_shapes=[
            pltpu.VMEM((SPAN, 2 * PAD), bf16),
            pltpu.VMEM((TILE, WINDOW), f32),
            dma((4,)),
        ],
        name="attend",
    )(qo, kvo)
    mg = pl.pallas_call(
        gather_kernel,
        out_shape=jax.ShapeDtypeStruct((16, ROWS, PAD), bf16),
        in_specs=[VM],
        out_specs=ANY,
        scratch_shapes=[dma((16,)), dma((16,)), dma],
        compiler_params=pltpu.CompilerParams(collective_id=2, has_side_effects=True),
        name="gather",
    )(mixed)
    y = pl.pallas_call(
        output_kernel,
        out_shape=jax.ShapeDtypeStruct((ROWS, PART), bf16),
        in_specs=[VM, ANY, VM],
        out_specs=VM,
        scratch_shapes=[
            pltpu.VMEM((WIDTH, PART), bf16),
            pltpu.VMEM((16 * PAD, PART), bf16),
            dma,
        ],
        name="output",
    )(mg, w_out, wg)
    return (y, cache)


def solution(mesh):
    return jax.shard_map(
        shards,
        mesh=mesh,
        in_specs=(
            P("seq", "tp"),
            P(),
            P(None, None, "tp"),
            P("tp", None),
            P("tp"),
            P("seq"),
            P("seq"),
            P("seq"),
        ),
        out_specs=(P("seq", "tp"), P(None, "seq", "tp")),
        check_vma=False,
    )
```

```python
import functools
import math

import jax
import jax.numpy as jnp
from jax import lax
from jax.experimental import pallas as pl
from jax.experimental.pallas import tpu as pltpu
from jax.sharding import PartitionSpec as P

WINDOW = 4096
SINKS = 4
EPS = 1e-05
THETA = 10000.0
LONG = 32832

ROWS = 576
MODEL = 3072
PART = 768
WIDTH = 384
HD = 96
PAD = 128
GROUP = 2304
TILE = 256
CHUNK = 144
STEPS = 4
PREV1 = GROUP
OWN = 2 * GROUP
SINK_AT = 3 * GROUP
SPAN = 3 * GROUP + 16
FAR = 512
NEG = -1e30
MESH = pl.DeviceIdType.MESH
ANY = pl.BlockSpec(memory_space=pl.ANY)
VM = pl.BlockSpec(memory_space=pltpu.VMEM)


def place():
    seq = lax.axis_index("seq")
    tp = lax.axis_index("tp")
    return seq, tp, tp // 2, tp % 2


def remote(src, dst, send, recv, seq, tp):
    return pltpu.make_async_remote_copy(
        src_ref=src,
        dst_ref=dst,
        send_sem=send,
        recv_sem=recv,
        device_id=(seq, tp),
        device_id_type=MESH,
    )


def greet(seq, tp):
    pl.semaphore_signal(
        pltpu.get_barrier_semaphore(), inc=1, device_id=(seq, tp), device_id_type=MESH
    )


def lanes(rows):
    return lax.broadcasted_iota(jnp.int32, (rows, PAD), 1)


def project_kernel(
    x_ref, gain_ref, w_ref, cos_ref, sin_ref, kmark_ref, qmark_ref, sink_ref, wo_ref,
    q_ref, kv_ref, cache_ref, wg_ref,
    held, weights, acc, square, wsem, xsem, send, recv, wsend, wrecv,
):
    seq, tp, yl, core = place()
    mate = yl * 2 + 1 - core
    cross = (1 - yl) * 2 + core
    far = (1 - yl) * 2 + 1 - core
    flipped = seq + 1 - 2 * (seq % 2)
    order = (tp, mate, cross, far)
    own = pltpu.make_async_copy(x_ref, held.at[0], xsem)
    own.start()

    def weight_copy(k):
        start = pl.multiple_of(order[k] * PART, PART)
        return pltpu.make_async_copy(
            w_ref.at[:, pl.ds(start, PART), :], weights.at[k], wsem.at[k]
        )

    for k in range(4):
        weight_copy(k).start()
    greet(seq, mate)
    greet(seq, cross)
    greet(flipped, cross)
    greet(flipped, far)
    pl.semaphore_wait(pltpu.get_barrier_semaphore(), 4)

    def part(c):
        return pl.ds(pl.multiple_of(c * CHUNK, CHUNK), CHUNK)

    def to_cross(c):
        return remote(x_ref.at[part(c)], held.at[2, part(c)], send.at[c], recv.at[c], seq, cross)

    @pl.loop(0, STEPS)
    def _(c):
        to_cross(c).start()

    to_mate = remote(x_ref, held.at[1], send.at[8], recv.at[8], seq, mate)
    to_mate.start()

    def block(k, c):
        rows = part(c)
        x = held[k, rows, :].astype(jnp.float32)
        sums = jnp.sum(x * x, axis=-1, keepdims=True)
        y = (x * gain_ref[order[k]]).astype(jnp.bfloat16)
        if k == 0:
            square[rows, :] = sums
        else:
            square[rows, :] += sums
        for j in range(3):
            cols = pl.ds(j * WIDTH, WIDTH)
            term = jnp.dot(y, weights[k, j], preferred_element_type=jnp.float32)
            if k == 0:
                acc[rows, cols] = term
            else:
                acc[rows, cols] += term

    def close(c):
        rows = part(c)
        lane = lanes(CHUNK)
        factor = lax.rsqrt(square[rows, :] / MODEL + EPS)
        kmark = kmark_ref[rows, :]
        qmark = qmark_ref[rows, :]
        valid = 1.0 - kmark[:, 100:101]
        cosine = cos_ref[rows, :]
        sine = sin_ref[rows, :]

        def heads(j):
            b = [acc[rows, pl.ds(j * WIDTH + n * PAD, PAD)] * factor for n in range(3)]
            return b, [
                b[0],
                jnp.where(lane < 32, pltpu.roll(b[0], 32, 1), pltpu.roll(b[1], 32, 1)),
                jnp.where(lane < 64, pltpu.roll(b[1], 64, 1), pltpu.roll(b[2], 64, 1)),
                pltpu.roll(b[2], 96, 1),
            ]

        def turn(u):
            other = jnp.where(lane < 48, pltpu.roll(u, 80, 1), pltpu.roll(u, 48, 1))
            return jnp.where(lane < HD, u * cosine + other * sine, 0.0)

        for h, u in enumerate(heads(0)[1]):
            full = turn(u) * (HD ** -0.5 / math.log(2.0)) + qmark + sink_ref[h]
            q_ref[h, rows, :] = full.astype(jnp.bfloat16)
        keys = []
        for h, u in enumerate(heads(1)[1]):
            k = turn(u)
            keys.append(k)
            kv_ref[h, rows, 0:PAD] = (k + kmark).astype(jnp.bfloat16)
        k1, k2, k3 = (pltpu.roll(keys[1], 96, 1), pltpu.roll(keys[2], 64, 1), pltpu.roll(keys[3], 32, 1))
        joined = (
            jnp.where(lane < 96, keys[0], k1),
            jnp.where(lane < 64, k1, k2),
            jnp.where(lane < 32, k2, k3),
        )
        plain, values = heads(2)
        for n in range(3):
            cols = pl.ds(n * PAD, PAD)
            cache_ref[0, rows, cols] = (joined[n] * valid).astype(jnp.bfloat16)
            cache_ref[1, rows, cols] = (plain[n] * valid).astype(jnp.bfloat16)
        for h, u in enumerate(values):
            v = jnp.where(lane < HD, u, jnp.where(lane == HD, 1.0, 0.0))
            kv_ref[h, rows, PAD:] = v.astype(jnp.bfloat16)

    def wide(t):
        return pl.ds(pl.multiple_of(t * PART, PART), PART)

    slabs = [
        remote(wo_ref.at[:, wide(t2)], wg_ref.at[n], wsend.at[n], wrecv.at[n], s2, t2)
        for n, (s2, t2) in enumerate(((seq, mate), (flipped, cross), (flipped, far)))
    ]
    for copy in slabs:
        copy.start()

    own.wait()
    weight_copy(0).wait()

    @pl.loop(0, STEPS)
    def _(c):
        block(0, c)

    to_mate.wait_recv()
    weight_copy(1).wait()

    @pl.loop(0, STEPS)
    def _(c):
        block(1, c)

    weight_copy(2).wait()
    weight_copy(3).wait()

    def onward(c):
        return remote(
            held.at[2, part(c)], held.at[3, part(c)], send.at[4 + c], recv.at[4 + c], seq, mate
        )

    @pl.loop(0, STEPS + 1)
    def _(c):
        @pl.when(c < STEPS)
        def _():
            to_cross(c).wait_recv()
            onward(c).start()
            block(2, c)

        @pl.when(c > 0)
        def _():
            onward(c - 1).wait_recv()
            block(3, c - 1)
            close(c - 1)

    @pl.loop(0, STEPS)
    def _(c):
        to_cross(c).wait_send()
        onward(c).wait_send()

    to_mate.wait_send()
    for copy in slabs:
        copy.wait()


def exchange_kernel(
    q_ref, kv_ref, qo_ref, kvo_ref,
    a_send, a_recv, b_send, b_recv, x_send, z_send, one_recv, two_recv, s_send, s_recv,
):
    seq, tp, yl, core = place()
    group = seq // 4
    m = seq % 4
    z = seq // 8
    xp = group % 2
    xb = m // 2
    hy = m % 2
    hx = xb + xp - 2 * xp * xb
    cross = (1 - yl) * 2 + core
    beside = 4 * (group + 1 - 2 * xp) + (1 - xb) * 2 + hy
    root = hx * 2 + hy

    def holder(g):
        odd = g % 2
        return 4 * g + (hx + odd - 2 * odd * hx) * 2 + hy

    for d in range(4):
        greet(4 * group + d, cross)
    greet(beside, tp)

    @pl.when(z > 0)
    def _():
        greet(seq - 8, tp)

    @pl.when(z < 7)
    def _():
        greet(seq + 8, tp)

    @pl.when(group == 0)
    def _():
        @pl.loop(1, 16)
        def _(g):
            greet(holder(g), tp)

    @pl.when(group > 0)
    def _():
        greet(root, tp)

    count = 5 + jnp.where(z > 0, 1, 0) + jnp.where(z < 7, 1, 0) + jnp.where(group == 0, 15, 1)
    pl.semaphore_wait(pltpu.get_barrier_semaphore(), count)

    def piece(base, s, c):
        return pl.ds(pl.multiple_of(base + s * ROWS + c * CHUNK, 16), CHUNK)

    def head_of(d):
        b = d // 2
        return (b + xp - 2 * xp * b) * 2 + d % 2

    def spread(d, c):
        return remote(
            kv_ref.at[head_of(d), piece(0, 0, c)], kvo_ref.at[piece(OWN, m, c)],
            a_send.at[d, c], a_recv.at[m, c], 4 * group + d, cross,
        )

    def spread_q(d):
        return remote(
            q_ref.at[head_of(d)], qo_ref.at[pl.ds(pl.multiple_of(m * ROWS, 64), ROWS)],
            b_send.at[d], b_recv.at[m], 4 * group + d, cross,
        )

    for c in range(STEPS):
        for d in range(4):
            spread(d, c).start()
    for d in range(4):
        spread_q(d).start()

    def arrived(ref, sem):
        pltpu.make_async_copy(ref, ref, sem).wait()

    def across(s, c):
        return remote(
            kvo_ref.at[piece(OWN, s, c)], kvo_ref.at[piece(PREV1, s, c)],
            x_send.at[s, c], one_recv.at[s, c], beside, tp,
        )

    def passed(s, c):
        return remote(
            kvo_ref.at[piece(0, s, c)], kvo_ref.at[piece(PREV1, s, c)],
            x_send.at[s, c], one_recv.at[s, c], beside, tp,
        )

    def ahead(s, c):
        return remote(
            kvo_ref.at[piece(OWN, s, c)], kvo_ref.at[piece(0, s, c)],
            z_send.at[s, c], two_recv.at[s, c], seq + 8, tp,
        )

    def sink_copy(g):
        return remote(
            kvo_ref.at[pl.ds(OWN, 16)], kvo_ref.at[pl.ds(SINK_AT, 16)], s_send.at[g], s_recv, holder(g), tp
        )

    def needed(s, c):
        return (xp == 1) | (s > 0) | (c == STEPS - 1)

    @pl.loop(0, 20)
    def _(n):
        c = n // 4
        s = n % 4

        @pl.when(n < 16)
        def _():
            arrived(kvo_ref.at[piece(OWN, s, c)], a_recv.at[s, c])

            @pl.when(xp == 0)
            def _():
                across(s, c).start()

            @pl.when((z < 7) & needed(s, c))
            def _():
                ahead(s, c).start()

        @pl.when((n == 0) & (group == 0))
        def _():
            @pl.loop(1, 16)
            def _(g):
                sink_copy(g).start()

        @pl.when((n >= 4) & (xp == 1) & (z > 0))
        def _():
            arrived(kvo_ref.at[piece(0, s, c - 1)], two_recv.at[s, c - 1])
            passed(s, c - 1).start()

    @pl.loop(0, 16)
    def _(n):
        c = n // 4
        s = n % 4

        @pl.when((xp == 0) & (z > 0) & needed(s, c))
        def _():
            arrived(kvo_ref.at[piece(0, s, c)], two_recv.at[s, c])

        @pl.when((xp == 1) | (z > 0))
        def _():
            arrived(kvo_ref.at[piece(PREV1, s, c)], one_recv.at[s, c])

    @pl.when(group > 0)
    def _():
        arrived(kvo_ref.at[pl.ds(SINK_AT, 16)], s_recv)

    for s in range(4):
        arrived(qo_ref.at[pl.ds(s * ROWS, ROWS)], b_recv.at[s])
    for d in range(4):
        spread_q(d).wait_send()

    @pl.loop(0, 16)
    def _(n):
        c = n // 4
        s = n % 4
        spread(s, c).wait_send()

        @pl.when(xp == 0)
        def _():
            across(s, c).wait_send()

        @pl.when((xp == 1) & (z > 0))
        def _():
            passed(s, c).wait_send()

        @pl.when((z < 7) & needed(s, c))
        def _():
            ahead(s, c).wait_send()

    @pl.when(group == 0)
    def _():
        @pl.loop(1, 16)
        def _(g):
            sink_copy(g).wait_send()


def dot_t(a, b):
    return lax.dot_general(a, b, (((1,), (1,)), ((), ())), preferred_element_type=jnp.float32)


def attend_kernel(
    q_ref, kvh_ref, wo_ref, wg_ref, y_ref,
    kv, scores, o_ref, mixed, slab, padded, sem, send, recv, pass_send, lsem,
):
    seq, tp, yl, core = place()
    group = seq // 4
    m = seq % 4
    xp = group % 2
    mate = yl * 2 + 1 - core
    order = (tp, mate, (1 - yl) * 2 + core, (1 - yl) * 2 + 1 - core)
    greet(seq, mate)
    for d in range(4):
        for low in range(2):
            @pl.when((m != d) | (yl != low))
            def _():
                greet(4 * group + d, low * 2 + core)
    own_slab = pltpu.make_async_copy(wo_ref.at[:, pl.ds(pl.multiple_of(tp * PART, PART), PART)], slab, sem.at[4])
    own_slab.start()

    def load(start, size, n):
        return pltpu.make_async_copy(
            kvh_ref.at[pl.ds(start, size)], kv.at[pl.ds(start, size)], sem.at[n]
        )

    def blank(start, size):
        mark = lax.broadcasted_iota(jnp.int32, (16, 2 * PAD), 1)
        row = jnp.where(mark == 102, 1.0, 0.0).astype(jnp.bfloat16)

        @pl.loop(0, size // 16)
        def _(n):
            kv[pl.ds(pl.multiple_of(start + n * 16, 16), 16), :] = row

    pieces = ((OWN, GROUP, 0), (PREV1, GROUP, 1), (FAR, GROUP - FAR, 2), (SINK_AT, 16, 1))
    for n, (start, size, least) in enumerate(pieces):
        @pl.when(group >= least)
        def _():
            load(start, size, n).start()

        @pl.when(group < least)
        def _():
            blank(start, size)

    for n in range(16):
        padded[pl.ds(n * PAD + HD, PAD - HD), :] = jnp.zeros((PAD - HD, PART), jnp.bfloat16)
    for n in range(12):
        padded[pl.ds((n + 4) * PAD, HD), :] = wg_ref[n // 4, pl.ds(n % 4 * HD, HD), :]
    own_slab.wait()
    for n in range(4):
        padded[pl.ds(n * PAD, HD), :] = slab[pl.ds(n * HD, HD), :]
    for n, (start, size, least) in enumerate(pieces):
        @pl.when(group >= least)
        def _():
            load(start, size, n).wait()

    pl.semaphore_wait(pltpu.get_barrier_semaphore(), 8)

    def key(start, size):
        return kv[pl.ds(pl.multiple_of(start, TILE), size), 0:PAD]

    def val(start, size):
        return kv[pl.ds(pl.multiple_of(start, TILE), size), PAD:]

    down = lax.broadcasted_iota(jnp.int32, (TILE, TILE), 0)
    right = lax.broadcasted_iota(jnp.int32, (TILE, TILE), 1)
    lower = right <= down
    sink_k = kv[pl.ds(SINK_AT, 16), 0:PAD]
    sink_v = kv[pl.ds(SINK_AT, 16), PAD:]
    small_down = lax.broadcasted_iota(jnp.int32, (TILE, 16), 0)
    small_right = lax.broadcasted_iota(jnp.int32, (TILE, 16), 1)

    def finish(rows, acc):
        lane = lanes(TILE)
        out = acc * (1.0 / acc[:, HD:HD + 1])
        o_ref[rows, :] = jnp.where(lane < HD, out, 0.0).astype(jnp.bfloat16)

    def long_tile(i, rows, first):
        q = q_ref[rows, :]
        near = OWN + i * TILE
        outer = FAR + i * TILE
        s = jnp.where(lower, dot_t(q, key(near, TILE)), dot_t(q, key(outer, TILE)))
        scores[:, 0:TILE] = s
        top = jnp.maximum(s[:, :PAD], s[:, PAD:])
        distance = first + small_down - small_right
        seen = (small_right < SINKS) & (distance >= WINDOW)
        sink_s = jnp.where(seen, dot_t(q, sink_k), NEG)
        for c in range(5):
            s = dot_t(q, key(outer + TILE + c * 768, 768))
            scores[:, pl.ds(TILE + c * 768, 768)] = s
            for n in range(6):
                top = jnp.maximum(top, s[:, n * PAD:(n + 1) * PAD])
        peak = jnp.maximum(
            jnp.max(top, axis=-1, keepdims=True), jnp.max(sink_s, axis=-1, keepdims=True)
        )
        w = jnp.where(seen, jnp.exp2(sink_s - peak), 0.0).astype(jnp.bfloat16)
        acc = jnp.dot(w, sink_v, preferred_element_type=jnp.float32)
        w = jnp.exp2(scores[:, 0:TILE] - peak)
        acc += jnp.dot(
            jnp.where(lower, w, 0.0).astype(jnp.bfloat16), val(near, TILE), preferred_element_type=jnp.float32
        )
        acc += jnp.dot(
            jnp.where(lower, 0.0, w).astype(jnp.bfloat16), val(outer, TILE), preferred_element_type=jnp.float32
        )
        for c in range(5):
            w = jnp.exp2(scores[:, pl.ds(TILE + c * 768, 768)] - peak).astype(jnp.bfloat16)
            acc += jnp.dot(w, val(outer + TILE + c * 768, 768), preferred_element_type=jnp.float32)
        finish(rows, acc)

    def mixed_tile(i, rows, first):
        q = q_ref[rows, :]
        lane = lanes(TILE)
        qf = q.astype(jnp.float32)
        mine = qf[:, 101:102]
        pick = jnp.where(lane == 96, -1.0, jnp.where(lane == 97, mine, 0.0)).astype(jnp.bfloat16)
        lost = jnp.where(lane == 100, 1.0, 0.0).astype(jnp.bfloat16)
        distance = first + small_down - small_right
        seen = (small_right < SINKS) & (distance >= WINDOW) & (dot_t(pick, sink_k) == 0.0)
        sink_s = jnp.where(seen, dot_t(q, sink_k), NEG)
        peak = jnp.max(sink_s, axis=-1, keepdims=True)
        w = jnp.where(seen, jnp.exp2(sink_s - peak), 0.0).astype(jnp.bfloat16)
        acc = jnp.dot(w, sink_v, preferred_element_type=jnp.float32)
        low = jnp.where(first >= LONG, 15, 0)

        def step(n, carry):
            peak, acc = carry
            start = FAR + i * TILE + n * TILE
            k = key(start, TILE)
            gap = (16 - n) * TILE + down - right
            bad = dot_t(lost, k)
            seen = (gap >= 0) & (gap < WINDOW) & (dot_t(pick, k) == 0.0) & ((bad < 0.5) | (gap == 0))
            s = jnp.where(seen, dot_t(q, k), NEG)
            now = jnp.maximum(peak, jnp.max(s, axis=-1, keepdims=True))
            w = jnp.where(seen, jnp.exp2(s - now), 0.0).astype(jnp.bfloat16)
            acc = acc * jnp.exp2(peak - now) + jnp.dot(w, val(start, TILE), preferred_element_type=jnp.float32)
            return now, acc

        peak, acc = lax.fori_loop(low, 17, step, (peak, acc))
        finish(rows, acc)

    def head(member, low, who):
        b = member // 2
        return 4 * ((1 - low) * 2 + who) + (b + xp - 2 * xp * b) * 2 + member % 2

    mine = head(m, yl, core)
    halves = (pl.ds(0, 320), pl.ds(320, 256))

    def out(d, half, low):
        source = pl.ds(pl.multiple_of(d * ROWS + half * 320, 64), 256 if half else 320)
        return remote(
            o_ref.at[source], mixed.at[mine, halves[half]],
            send.at[d, half, low], recv.at[mine, half], 4 * group + d, low * 2 + core,
        )

    def local(d, half):
        source = pl.ds(pl.multiple_of(d * ROWS + half * 320, 64), 256 if half else 320)
        return pltpu.make_async_copy(o_ref.at[source], mixed.at[mine, halves[half]], lsem.at[half])

    def onward(d, half, low):
        g = head(d, low, core)
        ref = mixed.at[g, halves[half]]
        return remote(ref, ref, pass_send.at[d, half, low], recv.at[g, half], seq, mate)

    def arrived(g, half):
        ref = mixed.at[g, halves[half]]
        pltpu.make_async_copy(ref, ref, recv.at[g, half]).wait()

    def give(d, half):
        for low in range(2):
            @pl.when((m != d) | (yl != low))
            def _():
                out(d, half, low).start()

            @pl.when((m == d) & (yl == low))
            def _():
                local(d, half).start()

    def relay(half):
        for d in range(4):
            for low in range(2):
                @pl.when((m != d) | (yl != low))
                def _():
                    arrived(head(d, low, core), half)

                @pl.when((m == d) & (yl == low))
                def _():
                    local(d, half).wait()

                onward(d, half, low).start()

    tiles = GROUP // TILE

    @pl.loop(0, tiles + 1)
    def _(i):
        rows = pl.ds(pl.multiple_of(jnp.minimum(i, tiles - 1) * TILE, TILE), TILE)
        first = group * GROUP + i * TILE

        @pl.when((i < tiles) & (first + TILE <= LONG))
        def _():
            long_tile(i, rows, first)

        @pl.when((i < tiles) & (first + TILE > LONG))
        def _():
            mixed_tile(i, rows, first)

        for half in range(2):
            @pl.when((i > 0) & (i < tiles) & ((i + 1) % 2 == half))
            def _():
                give((i - 1) // 2, half)

            @pl.when((i > 1) & (i - 2 == 2 * m + half))
            def _():
                relay(half)

    partner = 1 - core
    for half in range(2):
        for d in range(4):
            for low in range(2):
                arrived(head(d, low, partner), half)
        size = 160 - 32 * half
        for n in range(2):
            rows = pl.ds(half * 320 + n * size, size)
            left = jnp.concatenate(
                [mixed[4 * order[k // 4] + k % 4, rows, :] for k in range(16)], axis=1
            )
            y_ref[rows, :] = jnp.dot(
                left, padded[...], preferred_element_type=jnp.float32
            ).astype(jnp.bfloat16)
    for d in range(4):
        for half in range(2):
            for low in range(2):
                @pl.when((m != d) | (yl != low))
                def _():
                    out(d, half, low).wait_send()

                onward(d, half, low).wait_send()


def shards(tokens, norm_gain, w_qkv, w_out, sink_logit, segment_ids, positions, padding_mask):
    bf16, f32 = jnp.bfloat16, jnp.float32
    spot = jnp.arange(PAD, dtype=jnp.int32)
    freq = THETA ** (-((spot % 48).astype(f32) * 2.0 / HD))
    angle = positions.astype(f32)[:, None] * freq[None, :]
    cosine = jnp.cos(angle)
    sine = jnp.where(spot[None, :] < 48, -jnp.sin(angle), jnp.sin(angle))
    seg = segment_ids.astype(f32)[:, None]
    sinkish = (positions < SINKS).astype(f32)[:, None]
    lost = 1.0 - padding_mask.astype(f32)[:, None]
    kmark = jnp.where(spot == 96, seg, 0.0) + jnp.where(spot == 97, 1.0, 0.0)
    kmark = kmark + jnp.where((spot == 98) | (spot == 99), sinkish, 0.0) + jnp.where(spot == 100, lost, 0.0)
    qmark = jnp.where(spot == 101, seg, 0.0) + jnp.where(spot == 102, NEG, 0.0)
    logit = sink_logit * (1.0 / math.log(2.0))
    high = lax.reduce_precision(logit, 8, 7)
    low = logit - high
    sink = jnp.where(spot == 98, high[:, None], 0.0) + jnp.where(spot == 99, low[:, None], 0.0)
    sink = sink.reshape(4, 1, PAD)

    dma = pltpu.SemaphoreType.DMA
    q, kv, cache, wg = pl.pallas_call(
        project_kernel,
        out_shape=(
            jax.ShapeDtypeStruct((4, ROWS, PAD), bf16),
            jax.ShapeDtypeStruct((4, ROWS, 2 * PAD), bf16),
            jax.ShapeDtypeStruct((2, ROWS, WIDTH), bf16),
            jax.ShapeDtypeStruct((3, WIDTH, PART), bf16),
        ),
        in_specs=[ANY, VM, ANY, VM, VM, VM, VM, VM, ANY],
        out_specs=(VM, VM, VM, ANY),
        scratch_shapes=[
            pltpu.VMEM((4, ROWS, PART), bf16),
            pltpu.VMEM((4, 3, PART, WIDTH), bf16),
            pltpu.VMEM((ROWS, 3 * WIDTH), f32),
            pltpu.VMEM((ROWS, 1), f32),
            dma((4,)),
            dma,
            dma((9,)),
            dma((9,)),
            dma((3,)),
            dma((3,)),
        ],
        compiler_params=pltpu.CompilerParams(collective_id=0, has_side_effects=True),
        name="project",
    )(
        tokens, norm_gain.reshape(4, 1, PART), jnp.transpose(w_qkv, (1, 0, 2)),
        cosine, sine, kmark, qmark, sink, w_out,
    )
    qo, kvo = pl.pallas_call(
        exchange_kernel,
        out_shape=(
            jax.ShapeDtypeStruct((GROUP, PAD), bf16),
            jax.ShapeDtypeStruct((SPAN, 2 * PAD), bf16),
        ),
        in_specs=[ANY, ANY],
        out_specs=(ANY, ANY),
        scratch_shapes=[
            dma((4, 4)), dma((4, 4)), dma((4,)), dma((4,)), dma((4, 4)), dma((4, 4)),
            dma((4, 4)), dma((4, 4)), dma((16,)), dma,
        ],
        compiler_params=pltpu.CompilerParams(collective_id=1, has_side_effects=True),
        name="exchange",
    )(q, kv)
    y = pl.pallas_call(
        attend_kernel,
        out_shape=jax.ShapeDtypeStruct((ROWS, PART), bf16),
        in_specs=[VM, ANY, ANY, VM],
        out_specs=VM,
        scratch_shapes=[
            pltpu.VMEM((SPAN, 2 * PAD), bf16),
            pltpu.VMEM((TILE, WINDOW), f32),
            pltpu.VMEM((GROUP, PAD), bf16),
            pltpu.VMEM((16, ROWS, PAD), bf16),
            pltpu.VMEM((WIDTH, PART), bf16),
            pltpu.VMEM((16 * PAD, PART), bf16),
            dma((5,)),
            dma((4, 2, 2)),
            dma((16, 2)),
            dma((4, 2, 2)),
            dma((2,)),
        ],
        compiler_params=pltpu.CompilerParams(collective_id=2, has_side_effects=True),
        name="attend",
    )(qo, kvo, w_out, wg)
    return (y, cache)


def solution(mesh):
    return jax.shard_map(
        shards,
        mesh=mesh,
        in_specs=(
            P("seq", "tp"),
            P(),
            P(None, None, "tp"),
            P("tp", None),
            P("tp"),
            P("seq"),
            P("seq"),
            P("seq"),
        ),
        out_specs=(P("seq", "tp"), P(None, "seq", "tp")),
        check_vma=False,
    )
```

```python
import math

import jax
import jax.numpy as jnp
import numpy as np
from jax import lax
from jax.experimental import pallas as pl
from jax.experimental.pallas import tpu as pltpu
from jax.sharding import PartitionSpec as P

WINDOW = 4096
SINKS = 4
EPS = 1e-05
THETA = 10000.0
LONG = 32832

ROWS = 576
MODEL = 3072
PART = 768
WIDTH = 384
HD = 96
PAD = 128
GROUP = 2304
TILE = 256
CHUNK = 144
STEPS = 4
PREV1 = GROUP
OWN = 2 * GROUP
SINK_AT = 3 * GROUP
SPAN = 3 * GROUP + 16
FAR = 512
NEG = -1e30
MESH = pl.DeviceIdType.MESH
ANY = pl.BlockSpec(memory_space=pl.ANY)
VM = pl.BlockSpec(memory_space=pltpu.VMEM)


def place():
    seq = lax.axis_index("seq")
    tp = lax.axis_index("tp")
    return seq, tp, tp // 2, tp % 2


def remote(src, dst, send, recv, seq, tp):
    return pltpu.make_async_remote_copy(
        src_ref=src,
        dst_ref=dst,
        send_sem=send,
        recv_sem=recv,
        device_id=(seq, tp),
        device_id_type=MESH,
    )


def arrived(ref, sem):
    pltpu.make_async_copy(ref, ref, sem).wait()


def greet(seq, tp):
    pl.semaphore_signal(
        pltpu.get_barrier_semaphore(), inc=1, device_id=(seq, tp), device_id_type=MESH
    )


def lanes(rows):
    return lax.broadcasted_iota(jnp.int32, (rows, PAD), 1)


def dot_t(a, b):
    return lax.dot_general(a, b, (((1,), (1,)), ((), ())), preferred_element_type=jnp.float32)


def whole_kernel(
    x_ref, gain_ref, w_ref, info_ref, freq_ref, logit_ref, wo_ref,
    y_ref, cache_ref,
    held, weights, acc, square, mark_s, q_s, kv_s, qo, kv, scores, o_ref, mixed, wg, slab, padded,
    wsem, xsem, send, recv, wsend, wrecv, a_send, a_recv, b_send, b_recv,
    x_send, z_send, one_recv, two_recv, s_send, s_recv, o_send, o_recv, pass_send, lsem,
):
    seq, tp, yl, core = place()
    group = seq // 4
    m = seq % 4
    z = seq // 8
    xp = group % 2
    xb = m // 2
    hy = m % 2
    mate = yl * 2 + 1 - core
    cross = (1 - yl) * 2 + core
    far = (1 - yl) * 2 + 1 - core
    flipped = seq + 1 - 2 * hy
    beside = 4 * (group + 1 - 2 * xp) + (1 - xb) * 2 + hy
    order = (tp, mate, cross, far)

    def wide(t):
        return pl.ds(pl.multiple_of(t * PART, PART), PART)

    own = pltpu.make_async_copy(x_ref, held.at[0], xsem)
    own.start()

    def weight_copy(k):
        return pltpu.make_async_copy(w_ref.at[:, wide(order[k]), :], weights.at[k], wsem.at[k])

    for k in range(4):
        weight_copy(k).start()
    own_slab = pltpu.make_async_copy(wo_ref.at[:, wide(tp)], slab, wsem.at[4])
    own_slab.start()

    greet(seq, mate)
    greet(flipped, far)
    greet(beside, tp)
    for d in range(4):
        for low in range(2):
            @pl.when((m != d) | (yl != low))
            def _():
                greet(4 * group + d, low * 2 + core)

    @pl.when(z > 0)
    def _():
        greet(seq - 8, tp)

    @pl.when(z < 7)
    def _():
        greet(seq + 8, tp)

    pl.semaphore_wait(
        pltpu.get_barrier_semaphore(), 10 + jnp.where(z > 0, 1, 0) + jnp.where(z < 7, 1, 0)
    )

    def part(c):
        return pl.ds(pl.multiple_of(c * CHUNK, CHUNK), CHUNK)

    def to_cross(c):
        return remote(x_ref.at[part(c)], held.at[2, part(c)], send.at[c], recv.at[c], seq, cross)

    def onward_x(c):
        return remote(
            held.at[2, part(c)], held.at[3, part(c)], send.at[4 + c], recv.at[4 + c], seq, mate
        )

    @pl.loop(0, STEPS)
    def _(c):
        to_cross(c).start()

    to_mate = remote(x_ref, held.at[1], send.at[8], recv.at[8], seq, mate)
    to_mate.start()
    slabs = [
        remote(wo_ref.at[:, wide(t2)], wg.at[n], wsend.at[n], wrecv.at[n], s2, t2)
        for n, (s2, t2) in enumerate(((seq, mate), (flipped, cross), (flipped, far)))
    ]
    for copy in slabs:
        copy.start()

    def blank(start, size):
        mark = lax.broadcasted_iota(jnp.int32, (16, 2 * PAD), 1)
        row = jnp.where(mark == 102, 1.0, 0.0).astype(jnp.bfloat16)

        @pl.loop(0, size // 16)
        def _(n):
            kv[pl.ds(pl.multiple_of(start + n * 16, 16), 16), :] = row

    @pl.when(group == 0)
    def _():
        blank(PREV1, GROUP)
        blank(SINK_AT, 16)

    @pl.when(group < 2)
    def _():
        blank(FAR, GROUP - FAR)

    lane_row = lanes(1)
    sinks = []
    for h in range(4):
        logit = jnp.full((1, PAD), logit_ref[h], jnp.float32) * (1.0 / math.log(2.0))
        high = logit.astype(jnp.bfloat16).astype(jnp.float32)
        sinks.append(jnp.where(lane_row == 98, high, jnp.where(lane_row == 99, logit - high, 0.0)))

    def tables(c):
        rows = part(c)
        lane = lanes(CHUNK)
        info = info_ref[rows, :]
        pos = info[:, 0:1]
        seg = info[:, 1:2]
        lost = 1.0 - info[:, 2:3]
        first = jnp.where(pos < SINKS, 1.0, 0.0)
        mark_s[0, rows, :] = jnp.where(
            lane == 96, seg,
            jnp.where(
                lane == 97, 1.0,
                jnp.where((lane == 98) | (lane == 99), first, jnp.where(lane == 100, lost, 0.0)),
            ),
        )
        mark_s[1, rows, :] = jnp.where(lane == 101, seg, jnp.where(lane == 102, NEG, 0.0))
        turns = pos * freq_ref[0:1, :]
        turns = (turns - jnp.round(turns)) + pos * freq_ref[1:2, :]
        angle = (turns - jnp.round(turns)) * (2.0 * math.pi)
        sine = jnp.sin(angle)
        mark_s[2, rows, :] = jnp.cos(angle)
        mark_s[3, rows, :] = jnp.where(lane < 48, -sine, sine)

    def block(k, c):
        rows = part(c)
        x = held[k, rows, :].astype(jnp.float32)
        sums = jnp.sum(x * x, axis=-1, keepdims=True)
        y = (x * gain_ref[:, wide(order[k])]).astype(jnp.bfloat16)
        if k == 0:
            square[rows, :] = sums
        else:
            square[rows, :] += sums
        for j in range(3):
            cols = pl.ds(j * WIDTH, WIDTH)
            term = jnp.dot(y, weights[k, j], preferred_element_type=jnp.float32)
            if k == 0:
                acc[rows, cols] = term
            else:
                acc[rows, cols] += term

    def close(c):
        rows = part(c)
        lane = lanes(CHUNK)
        factor = lax.rsqrt(square[rows, :] / MODEL + EPS)
        info = info_ref[rows, :]
        valid = info[:, 2:3]
        kmark = mark_s[0, rows, :]
        qmark = mark_s[1, rows, :]
        cosine = mark_s[2, rows, :]
        sine = mark_s[3, rows, :]

        def heads(j):
            b = [acc[rows, pl.ds(j * WIDTH + n * PAD, PAD)] * factor for n in range(3)]
            return b, [
                b[0],
                jnp.where(lane < 32, pltpu.roll(b[0], 32, 1), pltpu.roll(b[1], 32, 1)),
                jnp.where(lane < 64, pltpu.roll(b[1], 64, 1), pltpu.roll(b[2], 64, 1)),
                pltpu.roll(b[2], 96, 1),
            ]

        def turn(u):
            other = jnp.where(lane < 48, pltpu.roll(u, 80, 1), pltpu.roll(u, 48, 1))
            return jnp.where(lane < HD, u * cosine + other * sine, 0.0)

        for h, u in enumerate(heads(0)[1]):
            full = turn(u) * (HD ** -0.5 / math.log(2.0)) + qmark + sinks[h]
            q_s[h, rows, :] = full.astype(jnp.bfloat16)
        keys = []
        for h, u in enumerate(heads(1)[1]):
            k = turn(u)
            keys.append(k)
            kv_s[h, rows, 0:PAD] = (k + kmark).astype(jnp.bfloat16)
        k1, k2, k3 = (pltpu.roll(keys[1], 96, 1), pltpu.roll(keys[2], 64, 1), pltpu.roll(keys[3], 32, 1))
        joined = (
            jnp.where(lane < 96, keys[0], k1),
            jnp.where(lane < 64, k1, k2),
            jnp.where(lane < 32, k2, k3),
        )
        plain, values = heads(2)
        for n in range(3):
            cols = pl.ds(n * PAD, PAD)
            cache_ref[0, rows, cols] = (joined[n] * valid).astype(jnp.bfloat16)
            cache_ref[1, rows, cols] = (plain[n] * valid).astype(jnp.bfloat16)
        for h, u in enumerate(values):
            v = jnp.where(lane < HD, u, jnp.where(lane == HD, 1.0, 0.0))
            kv_s[h, rows, PAD:] = v.astype(jnp.bfloat16)

    def piece(base, s, c):
        return pl.ds(pl.multiple_of(base + s * ROWS + c * CHUNK, 16), CHUNK)

    def head_of(d):
        b = d // 2
        return (b + xp - 2 * xp * b) * 2 + d % 2

    def spread(d, c):
        return remote(
            kv_s.at[head_of(d), part(c)], kv.at[piece(OWN, m, c)],
            a_send.at[d, c], a_recv.at[m, c], 4 * group + d, cross,
        )

    def spread_q(d, c):
        return remote(
            q_s.at[head_of(d), part(c)], qo.at[piece(0, m, c)],
            b_send.at[d, c], b_recv.at[m, c], 4 * group + d, cross,
        )

    def across(s, c):
        return remote(
            kv.at[piece(OWN, s, c)], kv.at[piece(PREV1, s, c)],
            x_send.at[s, c], one_recv.at[s, c], beside, tp,
        )

    def passed(s, c):
        return remote(
            kv.at[piece(0, s, c)], kv.at[piece(PREV1, s, c)],
            x_send.at[s, c], one_recv.at[s, c], beside, tp,
        )

    def ahead(s, c):
        return remote(
            kv.at[piece(OWN, s, c)], kv.at[piece(0, s, c)],
            z_send.at[s, c], two_recv.at[s, c], seq + 8, tp,
        )

    sink_rows = kv.at[pl.ds(SINK_AT, 16)]
    sink_from = kv.at[pl.ds(pl.multiple_of(jnp.where(z == 0, OWN, SINK_AT), 16), 16)]
    sink_beside = remote(sink_from, sink_rows, s_send.at[0], s_recv, beside, tp)
    sink_ahead = remote(sink_from, sink_rows, s_send.at[1], s_recv, seq + 8, tp)

    def needed(s, c):
        return (xp == 1) | (s > 0) | (c == STEPS - 1)

    def serve(n):
        c = n // 4
        s = n % 4

        @pl.when(n < 16)
        def _():
            arrived(kv.at[piece(OWN, s, c)], a_recv.at[s, c])

            @pl.when(xp == 0)
            def _():
                across(s, c).start()

            @pl.when((z < 7) & needed(s, c))
            def _():
                ahead(s, c).start()

        @pl.when((n == z) & (xp == 0))
        def _():
            @pl.when(z > 0)
            def _():
                arrived(sink_rows, s_recv)

            sink_beside.start()

            @pl.when(z < 7)
            def _():
                sink_ahead.start()

        @pl.when((n >= 4) & (xp == 1) & (z > 0))
        def _():
            arrived(kv.at[piece(0, s, c - 1)], two_recv.at[s, c - 1])
            passed(s, c - 1).start()

    @pl.loop(0, STEPS)
    def _(c):
        tables(c)

    own.wait()
    weight_copy(0).wait()

    @pl.loop(0, STEPS)
    def _(c):
        block(0, c)

    to_mate.wait_recv()
    weight_copy(1).wait()

    @pl.loop(0, STEPS)
    def _(c):
        block(1, c)

    weight_copy(2).wait()
    weight_copy(3).wait()

    @pl.loop(0, STEPS + 1)
    def _(c):
        @pl.when(c < STEPS)
        def _():
            to_cross(c).wait_recv()
            onward_x(c).start()
            block(2, c)

        @pl.when(c > 0)
        def _():
            onward_x(c - 1).wait_recv()
            block(3, c - 1)
            close(c - 1)
            for d in range(4):
                spread(d, c - 1).start()
            for d in range(4):
                spread_q(d, c - 1).start()

        @pl.when(c > 2)
        def _():
            @pl.loop(0, 4)
            def _(n):
                serve((c - 3) * 4 + n)

    @pl.loop(8, 20)
    def _(n):
        serve(n)

    for copy in slabs:
        copy.wait_recv()
    own_slab.wait()
    for n in range(16):
        padded[pl.ds(n * PAD + HD, PAD - HD), :] = jnp.zeros((PAD - HD, PART), jnp.bfloat16)
    for n in range(12):
        padded[pl.ds((n + 4) * PAD, HD), :] = wg[n // 4, pl.ds(n % 4 * HD, HD), :]
    for n in range(4):
        padded[pl.ds(n * PAD, HD), :] = slab[pl.ds(n * HD, HD), :]

    @pl.loop(0, 16)
    def _(n):
        c = n // 4
        s = n % 4
        arrived(qo.at[piece(0, s, c)], b_recv.at[s, c])

        @pl.when((xp == 0) & (z > 0) & needed(s, c))
        def _():
            arrived(kv.at[piece(0, s, c)], two_recv.at[s, c])

        @pl.when((xp == 1) | (z > 0))
        def _():
            arrived(kv.at[piece(PREV1, s, c)], one_recv.at[s, c])

    @pl.when(xp == 1)
    def _():
        arrived(sink_rows, s_recv)

    def key(start, size):
        return kv[pl.ds(pl.multiple_of(start, TILE), size), 0:PAD]

    def val(start, size):
        return kv[pl.ds(pl.multiple_of(start, TILE), size), PAD:]

    down = lax.broadcasted_iota(jnp.int32, (TILE, TILE), 0)
    right = lax.broadcasted_iota(jnp.int32, (TILE, TILE), 1)
    lower = right <= down
    sink_k = kv[pl.ds(SINK_AT, 16), 0:PAD]
    sink_v = kv[pl.ds(SINK_AT, 16), PAD:]
    small_down = lax.broadcasted_iota(jnp.int32, (TILE, 16), 0)
    small_right = lax.broadcasted_iota(jnp.int32, (TILE, 16), 1)

    def finish(rows, acc):
        lane = lanes(TILE)
        out = acc * (1.0 / acc[:, HD:HD + 1])
        o_ref[rows, :] = jnp.where(lane < HD, out, 0.0).astype(jnp.bfloat16)

    def long_tile(i, rows, first):
        q = qo[rows, :]
        near = OWN + i * TILE
        outer = FAR + i * TILE
        s = jnp.where(lower, dot_t(q, key(near, TILE)), dot_t(q, key(outer, TILE)))
        scores[:, 0:TILE] = s
        top = jnp.maximum(s[:, :PAD], s[:, PAD:])
        distance = first + small_down - small_right
        seen = (small_right < SINKS) & (distance >= WINDOW)
        sink_s = jnp.where(seen, dot_t(q, sink_k), NEG)
        for c in range(5):
            s = dot_t(q, key(outer + TILE + c * 768, 768))
            scores[:, pl.ds(TILE + c * 768, 768)] = s
            for n in range(6):
                top = jnp.maximum(top, s[:, n * PAD:(n + 1) * PAD])
        peak = jnp.maximum(
            jnp.max(top, axis=-1, keepdims=True), jnp.max(sink_s, axis=-1, keepdims=True)
        )
        w = jnp.where(seen, jnp.exp2(sink_s - peak), 0.0).astype(jnp.bfloat16)
        acc = jnp.dot(w, sink_v, preferred_element_type=jnp.float32)
        w = jnp.exp2(scores[:, 0:TILE] - peak)
        acc += jnp.dot(
            jnp.where(lower, w, 0.0).astype(jnp.bfloat16), val(near, TILE), preferred_element_type=jnp.float32
        )
        acc += jnp.dot(
            jnp.where(lower, 0.0, w).astype(jnp.bfloat16), val(outer, TILE), preferred_element_type=jnp.float32
        )
        for c in range(5):
            w = jnp.exp2(scores[:, pl.ds(TILE + c * 768, 768)] - peak).astype(jnp.bfloat16)
            acc += jnp.dot(w, val(outer + TILE + c * 768, 768), preferred_element_type=jnp.float32)
        finish(rows, acc)

    def mixed_tile(i, rows, first):
        q = qo[rows, :]
        lane = lanes(TILE)
        qf = q.astype(jnp.float32)
        mine = qf[:, 101:102]
        pick = jnp.where(lane == 96, -1.0, jnp.where(lane == 97, mine, 0.0)).astype(jnp.bfloat16)
        lost = jnp.where(lane == 100, 1.0, 0.0).astype(jnp.bfloat16)
        distance = first + small_down - small_right
        seen = (small_right < SINKS) & (distance >= WINDOW) & (dot_t(pick, sink_k) == 0.0)
        sink_s = jnp.where(seen, dot_t(q, sink_k), NEG)
        peak = jnp.max(sink_s, axis=-1, keepdims=True)
        w = jnp.where(seen, jnp.exp2(sink_s - peak), 0.0).astype(jnp.bfloat16)
        acc = jnp.dot(w, sink_v, preferred_element_type=jnp.float32)
        low = jnp.where(first >= LONG, 15, 0)

        def step(n, carry):
            peak, acc = carry
            start = FAR + i * TILE + n * TILE
            k = key(start, TILE)
            gap = (16 - n) * TILE + down - right
            bad = dot_t(lost, k)
            seen = (gap >= 0) & (gap < WINDOW) & (dot_t(pick, k) == 0.0) & ((bad < 0.5) | (gap == 0))
            s = jnp.where(seen, dot_t(q, k), NEG)
            now = jnp.maximum(peak, jnp.max(s, axis=-1, keepdims=True))
            w = jnp.where(seen, jnp.exp2(s - now), 0.0).astype(jnp.bfloat16)
            acc = acc * jnp.exp2(peak - now) + jnp.dot(w, val(start, TILE), preferred_element_type=jnp.float32)
            return now, acc

        peak, acc = lax.fori_loop(low, 17, step, (peak, acc))
        finish(rows, acc)

    def head(member, low, who):
        b = member // 2
        return 4 * ((1 - low) * 2 + who) + (b + xp - 2 * xp * b) * 2 + member % 2

    mine = head(m, yl, core)
    outer = (m == 0) | (m == 3)
    begins = ((0, 192, 128, 320), (256, 0, 384, 64), (512, 448, 0, 0))
    turn_of = ((0, 2, 3, 1), (4, 6, 7, 5))
    parcels = (
        ((0, 0),), ((0, 1),), ((0, 2), (1, 1)), ((1, 0),), ((1, 2), (2, 2)),
        ((2, 0),), ((2, 1), (3, 2)), ((3, 1),), ((3, 0),),
    )
    sequence = (0, 8, 3, 5, 1, 7, 2, 6, 4)

    def size_of(d, p):
        return (256, 256, 64)[p] if d in (0, 3) else (256, 192, 128)[p]

    def pick_of(table, k):
        return jnp.where(k == 0, table[0], jnp.where(k == 1, table[1], jnp.where(k == 2, table[2], table[3])))

    def my_rows(p, size):
        return pl.ds(pl.multiple_of(pick_of(begins[p], m), 64), size)

    def out(d, p, low):
        size = size_of(d, p)
        return remote(
            o_ref.at[pl.ds(d * ROWS + begins[p][d], size)],
            mixed.at[mine, pl.ds(begins[p][d], size)],
            o_send.at[d, p, low], o_recv.at[mine, p], 4 * group + d, low * 2 + core,
        )

    def local(d, p):
        size = size_of(d, p)
        return pltpu.make_async_copy(
            o_ref.at[pl.ds(d * ROWS + begins[p][d], size)],
            mixed.at[mine, pl.ds(begins[p][d], size)], lsem.at[p],
        )

    def give(tile):
        for d, p in parcels[tile]:
            for low in range(2):
                @pl.when((m != d) | (yl != low))
                def _():
                    out(d, p, low).start()

                @pl.when((m == d) & (yl == low))
                def _():
                    local(d, p).start()

    def landed(g, p, size):
        arrived(mixed.at[g, my_rows(p, size)], o_recv.at[g, p])

    def onward(d, low, p, size):
        g = head(d, low, core)
        ref = mixed.at[g, my_rows(p, size)]
        return remote(ref, ref, pass_send.at[d, p, low], o_recv.at[g, p], seq, mate)

    def sized(p, body):
        if p == 0:
            body(256)
        else:
            @pl.when(outer)
            def _():
                body(size_of(0, p))

            @pl.when((m == 1) | (m == 2))
            def _():
                body(size_of(1, p))

    def relay(p):
        def body(size):
            for d in range(4):
                for low in range(2):
                    @pl.when((m != d) | (yl != low))
                    def _():
                        landed(head(d, low, core), p, size)

                    @pl.when((m == d) & (yl == low))
                    def _():
                        ref = mixed.at[mine, my_rows(p, size)]
                        arrived(ref, lsem.at[p])

                    onward(d, low, p, size).start()

        sized(p, body)

    tiles = GROUP // TILE

    @pl.loop(0, tiles)
    def _(n):
        i = jnp.int32(sequence[-1])
        for k in range(tiles - 1):
            i = jnp.where(n == k, sequence[k], i)
        rows = pl.ds(pl.multiple_of(i * TILE, TILE), TILE)
        first = group * GROUP + i * TILE

        @pl.when(first + TILE <= LONG)
        def _():
            long_tile(i, rows, first)

        @pl.when(first + TILE > LONG)
        def _():
            mixed_tile(i, rows, first)

        for tile in range(tiles):
            @pl.when(i == tile)
            def _():
                give(tile)

        for p in range(2):
            @pl.when(n == jnp.minimum(pick_of(turn_of[p], m) + 2, tiles - 1))
            def _():
                relay(p)

    partner = 1 - core

    def project_out(p):
        def body(size):
            for d in range(4):
                for low in range(2):
                    landed(head(d, low, partner), p, size)
            rows = my_rows(p, size)
            left = jnp.concatenate(
                [mixed[4 * order[k // 4] + k % 4, rows, :] for k in range(16)], axis=1
            )
            y_ref[rows, :] = jnp.dot(
                left, padded[...], preferred_element_type=jnp.float32
            ).astype(jnp.bfloat16)

        sized(p, body)

    project_out(0)
    relay(2)
    project_out(1)
    project_out(2)

    @pl.loop(0, STEPS)
    def _(c):
        to_cross(c).wait_send()
        onward_x(c).wait_send()

    to_mate.wait_send()
    for copy in slabs:
        copy.wait_send()

    @pl.loop(0, 16)
    def _(n):
        c = n // 4
        s = n % 4
        spread(s, c).wait_send()
        spread_q(s, c).wait_send()

        @pl.when(xp == 0)
        def _():
            across(s, c).wait_send()

        @pl.when((xp == 1) & (z > 0))
        def _():
            passed(s, c).wait_send()

        @pl.when((z < 7) & needed(s, c))
        def _():
            ahead(s, c).wait_send()

    @pl.when(xp == 0)
    def _():
        sink_beside.wait_send()

        @pl.when(z < 7)
        def _():
            sink_ahead.wait_send()

    for d in range(4):
        for p in range(3):
            for low in range(2):
                @pl.when((m != d) | (yl != low))
                def _():
                    out(d, p, low).wait_send()

    for p in range(3):
        def body(size):
            for d in range(4):
                for low in range(2):
                    onward(d, low, p, size).wait_send()

        sized(p, body)


def shards(tokens, norm_gain, w_qkv, w_out, sink_logit, segment_ids, positions, padding_mask):
    bf16, f32 = jnp.bfloat16, jnp.float32
    spot = jnp.arange(PAD, dtype=jnp.int32)[None, :]
    info = jnp.where(
        spot == 0, positions[:, None], jnp.where(spot == 1, segment_ids[:, None], padding_mask[:, None])
    ).astype(f32)
    turns = THETA ** (-(np.arange(PAD) % 48) * 2.0 / HD) / (2.0 * np.pi)
    scale = 2.0 ** (np.floor(np.log2(turns)) - 7.0)
    high = np.floor(turns / scale) * scale
    freq = np.zeros((8, PAD), np.float32)
    freq[0] = high
    freq[1] = turns - high

    dma = pltpu.SemaphoreType.DMA
    return pl.pallas_call(
        whole_kernel,
        out_shape=(
            jax.ShapeDtypeStruct((ROWS, PART), bf16),
            jax.ShapeDtypeStruct((2, ROWS, WIDTH), bf16),
        ),
        in_specs=[ANY, VM, ANY, VM, VM, pl.BlockSpec(memory_space=pltpu.SMEM), ANY],
        out_specs=(VM, VM),
        scratch_shapes=[
            pltpu.VMEM((4, ROWS, PART), bf16),
            pltpu.VMEM((4, 3, PART, WIDTH), bf16),
            pltpu.VMEM((ROWS, 3 * WIDTH), f32),
            pltpu.VMEM((ROWS, 1), f32),
            pltpu.VMEM((4, ROWS, PAD), f32),
            pltpu.VMEM((4, ROWS, PAD), bf16),
            pltpu.VMEM((4, ROWS, 2 * PAD), bf16),
            pltpu.VMEM((GROUP, PAD), bf16),
            pltpu.VMEM((SPAN, 2 * PAD), bf16),
            pltpu.VMEM((TILE, WINDOW), f32),
            pltpu.VMEM((GROUP, PAD), bf16),
            pltpu.VMEM((16, ROWS, PAD), bf16),
            pltpu.VMEM((3, WIDTH, PART), bf16),
            pltpu.VMEM((WIDTH, PART), bf16),
            pltpu.VMEM((16 * PAD, PART), bf16),
            dma((5,)), dma, dma((9,)), dma((9,)), dma((3,)), dma((3,)),
            dma((4, 4)), dma((4, 4)), dma((4, 4)), dma((4, 4)),
            dma((4, 4)), dma((4, 4)), dma((4, 4)), dma((4, 4)), dma((2,)), dma,
            dma((4, 3, 2)), dma((16, 3)), dma((4, 3, 2)), dma((3,)),
        ],
        compiler_params=pltpu.CompilerParams(
            collective_id=0, has_side_effects=True, vmem_limit_bytes=62 * 1024 * 1024
        ),
        name="whole",
    )(
        tokens, norm_gain.reshape(1, MODEL), jnp.transpose(w_qkv, (1, 0, 2)), info,
        jnp.asarray(freq), sink_logit, w_out,
    )


def solution(mesh):
    return jax.shard_map(
        shards,
        mesh=mesh,
        in_specs=(
            P("seq", "tp"),
            P(),
            P(None, None, "tp"),
            P("tp", None),
            P("tp"),
            P("seq"),
            P("seq"),
            P("seq"),
        ),
        out_specs=(P("seq", "tp"), P(None, "seq", "tp")),
        check_vma=False,
    )
```

```python
import math

import jax
import jax.numpy as jnp
import numpy as np
from jax import lax
from jax.experimental import pallas as pl
from jax.experimental.pallas import tpu as pltpu
from jax.sharding import PartitionSpec as P

WINDOW = 4096
SINKS = 4
EPS = 1e-05
THETA = 10000.0
LONG = 32832

ROWS = 576
MODEL = 3072
PART = 768
WIDTH = 384
HD = 96
PAD = 128
GROUP = 2304
TILE = 256
CHUNK = 144
STEPS = 4
PREV1 = GROUP
OWN = 2 * GROUP
SINK_AT = 3 * GROUP
SPAN = 3 * GROUP + 16
FAR = 512
NEG = -1e30
MESH = pl.DeviceIdType.MESH
ANY = pl.BlockSpec(memory_space=pl.ANY)
VM = pl.BlockSpec(memory_space=pltpu.VMEM)


def place():
    seq = lax.axis_index("seq")
    tp = lax.axis_index("tp")
    return seq, tp, tp // 2, tp % 2


def remote(src, dst, send, recv, seq, tp):
    return pltpu.make_async_remote_copy(
        src_ref=src,
        dst_ref=dst,
        send_sem=send,
        recv_sem=recv,
        device_id=(seq, tp),
        device_id_type=MESH,
    )


def arrived(ref, sem):
    pltpu.make_async_copy(ref, ref, sem).wait()


def greet(seq, tp):
    pl.semaphore_signal(
        pltpu.get_barrier_semaphore(), inc=1, device_id=(seq, tp), device_id_type=MESH
    )


def lanes(rows):
    return lax.broadcasted_iota(jnp.int32, (rows, PAD), 1)


def dot_t(a, b):
    return lax.dot_general(a, b, (((1,), (1,)), ((), ())), preferred_element_type=jnp.float32)


def whole_kernel(
    x_ref, gain_ref, w_ref, info_ref, freq_ref, logit_ref, wo_ref,
    y_ref, cache_ref,
    held, weights, acc, square, mark_s, q_s, kv_s, cache_s, qo, kv, scores_a, scores_b, peaks, o_ref, mixed, wg, slab, padded,
    wsem, xsem, send, recv, wsend, wrecv, a_send, a_recv, b_send, b_recv,
    x_send, z_send, one_recv, two_recv, s_send, s_recv, o_send, o_recv, pass_send, lsem, csem,
):
    scores = (scores_a, scores_b)
    seq, tp, yl, core = place()
    group = seq // 4
    m = seq % 4
    z = seq // 8
    xp = group % 2
    xb = m // 2
    hy = m % 2
    mate = yl * 2 + 1 - core
    cross = (1 - yl) * 2 + core
    far = (1 - yl) * 2 + 1 - core
    flipped = seq + 1 - 2 * hy
    beside = 4 * (group + 1 - 2 * xp) + (1 - xb) * 2 + hy
    order = (tp, mate, cross, far)

    def wide(t):
        return pl.ds(pl.multiple_of(t * PART, PART), PART)

    own = pltpu.make_async_copy(x_ref, held.at[0], xsem)
    own.start()

    def weight_copy(k):
        return pltpu.make_async_copy(w_ref.at[:, wide(order[k]), :], weights.at[k], wsem.at[k])

    for k in range(4):
        weight_copy(k).start()
    own_slab = pltpu.make_async_copy(wo_ref.at[:, wide(tp)], slab, wsem.at[4])
    own_slab.start()

    greet(seq, mate)
    greet(flipped, far)
    greet(beside, tp)
    for d in range(4):
        for low in range(2):
            @pl.when((m != d) | (yl != low))
            def _():
                greet(4 * group + d, low * 2 + core)

    @pl.when(z > 0)
    def _():
        greet(seq - 8, tp)

    @pl.when(z < 7)
    def _():
        greet(seq + 8, tp)

    pl.semaphore_wait(
        pltpu.get_barrier_semaphore(), 10 + jnp.where(z > 0, 1, 0) + jnp.where(z < 7, 1, 0)
    )

    def part(c):
        return pl.ds(pl.multiple_of(c * CHUNK, CHUNK), CHUNK)

    def to_cross(c):
        return remote(x_ref.at[part(c)], held.at[2, part(c)], send.at[c], recv.at[c], seq, cross)

    def onward_x(c):
        return remote(
            held.at[2, part(c)], held.at[3, part(c)], send.at[4 + c], recv.at[4 + c], seq, mate
        )

    @pl.loop(0, STEPS)
    def _(c):
        to_cross(c).start()

    to_mate = remote(x_ref, held.at[1], send.at[8], recv.at[8], seq, mate)
    to_mate.start()
    slabs = [
        remote(wo_ref.at[:, wide(t2)], wg.at[n], wsend.at[n], wrecv.at[n], s2, t2)
        for n, (s2, t2) in enumerate(((seq, mate), (flipped, cross), (flipped, far)))
    ]
    for copy in slabs:
        copy.start()

    def blank(start, size):
        mark = lax.broadcasted_iota(jnp.int32, (16, 2 * PAD), 1)
        row = jnp.where(mark == 102, 1.0, 0.0).astype(jnp.bfloat16)

        @pl.loop(0, size // 16)
        def _(n):
            kv[pl.ds(pl.multiple_of(start + n * 16, 16), 16), :] = row

    @pl.when(group == 0)
    def _():
        blank(PREV1, GROUP)
        blank(SINK_AT, 16)

    @pl.when(group < 2)
    def _():
        blank(FAR, GROUP - FAR)

    lane_row = lanes(1)
    sinks = []
    for h in range(4):
        logit = jnp.full((1, PAD), logit_ref[h], jnp.float32) * (1.0 / math.log(2.0))
        high = logit.astype(jnp.bfloat16).astype(jnp.float32)
        sinks.append(jnp.where(lane_row == 98, high, jnp.where(lane_row == 99, logit - high, 0.0)))

    def tables(c):
        rows = part(c)
        lane = lanes(CHUNK)
        info = info_ref[rows, :]
        pos = info[:, 0:1]
        seg = info[:, 1:2]
        lost = 1.0 - info[:, 2:3]
        first = jnp.where(pos < SINKS, 1.0, 0.0)
        mark_s[0, rows, :] = jnp.where(
            lane == 96, seg,
            jnp.where(
                lane == 97, 1.0,
                jnp.where((lane == 98) | (lane == 99), first, jnp.where(lane == 100, lost, 0.0)),
            ),
        )
        mark_s[1, rows, :] = jnp.where(lane == 101, seg, jnp.where(lane == 102, NEG, 0.0))
        turns = pos * freq_ref[0:1, :]
        turns = (turns - jnp.round(turns)) + pos * freq_ref[1:2, :]
        angle = (turns - jnp.round(turns)) * (2.0 * math.pi)
        sine = jnp.sin(angle)
        mark_s[2, rows, :] = jnp.cos(angle)
        mark_s[3, rows, :] = jnp.where(lane < 48, -sine, sine)

    def block(k, c):
        rows = part(c)
        x = held[k, rows, :].astype(jnp.float32)
        sums = jnp.sum(x * x, axis=-1, keepdims=True)
        y = (x * gain_ref[:, wide(order[k])]).astype(jnp.bfloat16)
        if k == 0:
            square[rows, :] = sums
        else:
            square[rows, :] += sums
        for j in range(3):
            cols = pl.ds(j * WIDTH, WIDTH)
            term = jnp.dot(y, weights[k, j], preferred_element_type=jnp.float32)
            if k == 0:
                acc[rows, cols] = term
            else:
                acc[rows, cols] += term

    def close(c):
        rows = part(c)
        lane = lanes(CHUNK)
        factor = lax.rsqrt(square[rows, :] / MODEL + EPS)
        info = info_ref[rows, :]
        valid = info[:, 2:3]
        kmark = mark_s[0, rows, :]
        qmark = mark_s[1, rows, :]
        cosine = mark_s[2, rows, :]
        sine = mark_s[3, rows, :]

        def heads(j):
            b = [acc[rows, pl.ds(j * WIDTH + n * PAD, PAD)] * factor for n in range(3)]
            return b, [
                b[0],
                jnp.where(lane < 32, pltpu.roll(b[0], 32, 1), pltpu.roll(b[1], 32, 1)),
                jnp.where(lane < 64, pltpu.roll(b[1], 64, 1), pltpu.roll(b[2], 64, 1)),
                pltpu.roll(b[2], 96, 1),
            ]

        def turn(u):
            other = jnp.where(lane < 48, pltpu.roll(u, 80, 1), pltpu.roll(u, 48, 1))
            return jnp.where(lane < HD, u * cosine + other * sine, 0.0)

        for h, u in enumerate(heads(0)[1]):
            full = turn(u) * (HD ** -0.5 / math.log(2.0)) + qmark + sinks[h]
            q_s[h, rows, :] = full.astype(jnp.bfloat16)
        keys = []
        for h, u in enumerate(heads(1)[1]):
            k = turn(u)
            keys.append(k)
            kv_s[h, rows, 0:PAD] = (k + kmark).astype(jnp.bfloat16)
        k1, k2, k3 = (pltpu.roll(keys[1], 96, 1), pltpu.roll(keys[2], 64, 1), pltpu.roll(keys[3], 32, 1))
        joined = (
            jnp.where(lane < 96, keys[0], k1),
            jnp.where(lane < 64, k1, k2),
            jnp.where(lane < 32, k2, k3),
        )
        plain, values = heads(2)
        for n in range(3):
            cols = pl.ds(n * PAD, PAD)
            cache_s[0, rows, cols] = joined[n] * valid
            cache_s[1, rows, cols] = plain[n] * valid
        for h, u in enumerate(values):
            v = jnp.where(lane < HD, u, jnp.where(lane == HD, 1.0, 0.0))
            kv_s[h, rows, PAD:] = v.astype(jnp.bfloat16)

    def piece(base, s, c):
        return pl.ds(pl.multiple_of(base + s * ROWS + c * CHUNK, 16), CHUNK)

    def head_of(d):
        b = d // 2
        return (b + xp - 2 * xp * b) * 2 + d % 2

    def spread(d, c):
        return remote(
            kv_s.at[head_of(d), part(c)], kv.at[piece(OWN, m, c)],
            a_send.at[d, c], a_recv.at[m, c], 4 * group + d, cross,
        )

    def spread_q(d, c):
        return remote(
            q_s.at[head_of(d), part(c)], qo.at[piece(0, m, c)],
            b_send.at[d, c], b_recv.at[m, c], 4 * group + d, cross,
        )

    def across(s, c):
        return remote(
            kv.at[piece(OWN, s, c)], kv.at[piece(PREV1, s, c)],
            x_send.at[s, c], one_recv.at[s, c], beside, tp,
        )

    def passed(s, c):
        return remote(
            kv.at[piece(0, s, c)], kv.at[piece(PREV1, s, c)],
            x_send.at[s, c], one_recv.at[s, c], beside, tp,
        )

    def ahead(s, c):
        return remote(
            kv.at[piece(OWN, s, c)], kv.at[piece(0, s, c)],
            z_send.at[s, c], two_recv.at[s, c], seq + 8, tp,
        )

    sink_rows = kv.at[pl.ds(SINK_AT, 16)]
    sink_from = kv.at[pl.ds(pl.multiple_of(jnp.where(z == 0, OWN, SINK_AT), 16), 16)]
    sink_beside = remote(sink_from, sink_rows, s_send.at[0], s_recv, beside, tp)
    sink_ahead = remote(sink_from, sink_rows, s_send.at[1], s_recv, seq + 8, tp)

    def needed(s, c):
        return (xp == 1) | (s > 0) | (c == STEPS - 1)

    def serve(n):
        c = n // 4
        s = n % 4

        @pl.when(n < 16)
        def _():
            arrived(kv.at[piece(OWN, s, c)], a_recv.at[s, c])

            @pl.when(xp == 0)
            def _():
                across(s, c).start()

            @pl.when((z < 7) & needed(s, c))
            def _():
                ahead(s, c).start()

        @pl.when((n == z) & (xp == 0))
        def _():
            @pl.when(z > 0)
            def _():
                arrived(sink_rows, s_recv)

            sink_beside.start()

            @pl.when(z < 7)
            def _():
                sink_ahead.start()

        @pl.when((n >= 4) & (xp == 1) & (z > 0))
        def _():
            arrived(kv.at[piece(0, s, c - 1)], two_recv.at[s, c - 1])
            passed(s, c - 1).start()

    @pl.loop(0, STEPS)
    def _(c):
        tables(c)

    own.wait()
    weight_copy(0).wait()

    @pl.loop(0, STEPS)
    def _(c):
        block(0, c)

    to_mate.wait_recv()
    weight_copy(1).wait()

    @pl.loop(0, STEPS)
    def _(c):
        block(1, c)

    weight_copy(2).wait()
    weight_copy(3).wait()

    @pl.loop(0, STEPS + 1)
    def _(c):
        @pl.when(c < STEPS)
        def _():
            to_cross(c).wait_recv()
            onward_x(c).start()
            block(2, c)

        @pl.when(c > 0)
        def _():
            onward_x(c - 1).wait_recv()
            block(3, c - 1)
            close(c - 1)
            for d in range(4):
                spread(d, c - 1).start()
            for d in range(4):
                spread_q(d, c - 1).start()

        @pl.when(c > 2)
        def _():
            @pl.loop(0, 4)
            def _(n):
                serve((c - 3) * 4 + n)

    cache_copy = pltpu.make_async_copy(cache_s, cache_ref, csem)
    cache_copy.start()

    @pl.loop(8, 20)
    def _(n):
        serve(n)

    for copy in slabs:
        copy.wait_recv()
    own_slab.wait()
    for n in range(16):
        padded[pl.ds(n * PAD + HD, PAD - HD), :] = jnp.zeros((PAD - HD, PART), jnp.bfloat16)
    for n in range(12):
        padded[pl.ds((n + 4) * PAD, HD), :] = wg[n // 4, pl.ds(n % 4 * HD, HD), :]
    for n in range(4):
        padded[pl.ds(n * PAD, HD), :] = slab[pl.ds(n * HD, HD), :]

    @pl.loop(0, 16)
    def _(n):
        c = n // 4
        s = n % 4
        arrived(qo.at[piece(0, s, c)], b_recv.at[s, c])

        @pl.when((xp == 0) & (z > 0) & needed(s, c))
        def _():
            arrived(kv.at[piece(0, s, c)], two_recv.at[s, c])

        @pl.when((xp == 1) | (z > 0))
        def _():
            arrived(kv.at[piece(PREV1, s, c)], one_recv.at[s, c])

    @pl.when(xp == 1)
    def _():
        arrived(sink_rows, s_recv)

    def key(start, size):
        return kv[pl.ds(pl.multiple_of(start, TILE), size), 0:PAD]

    def val(start, size):
        return kv[pl.ds(pl.multiple_of(start, TILE), size), PAD:]

    down = lax.broadcasted_iota(jnp.int32, (TILE, TILE), 0)
    right = lax.broadcasted_iota(jnp.int32, (TILE, TILE), 1)
    lower = right <= down
    sink_k = kv[pl.ds(SINK_AT, 16), 0:PAD]
    sink_v = kv[pl.ds(SINK_AT, 16), PAD:]
    small_down = lax.broadcasted_iota(jnp.int32, (TILE, 16), 0)
    small_right = lax.broadcasted_iota(jnp.int32, (TILE, 16), 1)

    def finish(rows, acc):
        lane = lanes(TILE)
        out = acc * (1.0 / acc[:, HD:HD + 1])
        o_ref[rows, :] = jnp.where(lane < HD, out, 0.0).astype(jnp.bfloat16)

    def sink_part(q, first):
        distance = first + small_down - small_right
        seen = (small_right < SINKS) & (distance >= WINDOW)
        return seen, jnp.where(seen, dot_t(q, sink_k), NEG)

    def score(i, slot):
        rows = pl.ds(pl.multiple_of(i * TILE, TILE), TILE)
        first = group * GROUP + i * TILE
        keep = scores[slot]
        q = qo[rows, :]
        near = OWN + i * TILE
        outer = FAR + i * TILE
        s = jnp.where(lower, dot_t(q, key(near, TILE)), dot_t(q, key(outer, TILE)))
        keep[:, 0:TILE] = s
        top = jnp.maximum(s[:, :PAD], s[:, PAD:])
        sink_s = sink_part(q, first)[1]
        for c in range(5):
            s = dot_t(q, key(outer + TILE + c * 768, 768))
            keep[:, pl.ds(TILE + c * 768, 768)] = s
            for n in range(6):
                top = jnp.maximum(top, s[:, n * PAD:(n + 1) * PAD])
        peaks[slot, :, :] = jnp.maximum(
            jnp.max(top, axis=-1, keepdims=True), jnp.max(sink_s, axis=-1, keepdims=True)
        )

    def weigh(i, slot):
        rows = pl.ds(pl.multiple_of(i * TILE, TILE), TILE)
        first = group * GROUP + i * TILE
        keep = scores[slot]
        q = qo[rows, :]
        near = OWN + i * TILE
        outer = FAR + i * TILE
        peak = peaks[slot, :, :]
        seen, sink_s = sink_part(q, first)
        w = jnp.where(seen, jnp.exp2(sink_s - peak), 0.0).astype(jnp.bfloat16)
        acc = jnp.dot(w, sink_v, preferred_element_type=jnp.float32)
        w = jnp.exp2(keep[:, 0:TILE] - peak)
        acc += jnp.dot(
            jnp.where(lower, w, 0.0).astype(jnp.bfloat16), val(near, TILE), preferred_element_type=jnp.float32
        )
        acc += jnp.dot(
            jnp.where(lower, 0.0, w).astype(jnp.bfloat16), val(outer, TILE), preferred_element_type=jnp.float32
        )
        for c in range(5):
            w = jnp.exp2(keep[:, pl.ds(TILE + c * 768, 768)] - peak).astype(jnp.bfloat16)
            acc += jnp.dot(w, val(outer + TILE + c * 768, 768), preferred_element_type=jnp.float32)
        finish(rows, acc)

    def mixed_tile(i, rows, first):
        q = qo[rows, :]
        lane = lanes(TILE)
        qf = q.astype(jnp.float32)
        mine = qf[:, 101:102]
        pick = jnp.where(lane == 96, -1.0, jnp.where(lane == 97, mine, 0.0)).astype(jnp.bfloat16)
        lost = jnp.where(lane == 100, 1.0, 0.0).astype(jnp.bfloat16)
        distance = first + small_down - small_right
        seen = (small_right < SINKS) & (distance >= WINDOW) & (dot_t(pick, sink_k) == 0.0)
        sink_s = jnp.where(seen, dot_t(q, sink_k), NEG)
        peak = jnp.max(sink_s, axis=-1, keepdims=True)
        w = jnp.where(seen, jnp.exp2(sink_s - peak), 0.0).astype(jnp.bfloat16)
        acc = jnp.dot(w, sink_v, preferred_element_type=jnp.float32)
        def step(n, carry):
            peak, acc = carry
            start = FAR + i * TILE + n * TILE
            k = key(start, TILE)
            gap = (16 - n) * TILE + down - right
            bad = dot_t(lost, k)
            seen = (gap >= 0) & (gap < WINDOW) & (dot_t(pick, k) == 0.0) & ((bad < 0.5) | (gap == 0))
            s = jnp.where(seen, dot_t(q, k), NEG)
            now = jnp.maximum(peak, jnp.max(s, axis=-1, keepdims=True))
            w = jnp.where(seen, jnp.exp2(s - now), 0.0).astype(jnp.bfloat16)
            acc = acc * jnp.exp2(peak - now) + jnp.dot(w, val(start, TILE), preferred_element_type=jnp.float32)
            return now, acc

        peak, acc = lax.fori_loop(15, 17, step, (peak, acc))
        out = acc * (1.0 / acc[:, HD:HD + 1])
        out = jnp.where(lane < HD, out, 0.0).astype(jnp.bfloat16)
        short = first + lax.broadcasted_iota(jnp.int32, (TILE, PAD), 0) >= LONG
        o_ref[rows, :] = jnp.where(short, out, o_ref[rows, :])

    def head(member, low, who):
        b = member // 2
        return 4 * ((1 - low) * 2 + who) + (b + xp - 2 * xp * b) * 2 + member % 2

    mine = head(m, yl, core)
    outer = (m == 0) | (m == 3)
    begins = ((0, 192, 128, 320), (256, 0, 384, 64), (512, 448, 0, 0))
    turn_of = ((0, 2, 3, 1), (4, 6, 7, 5))
    parcels = (
        ((0, 0),), ((0, 1),), ((0, 2), (1, 1)), ((1, 0),), ((1, 2), (2, 2)),
        ((2, 0),), ((2, 1), (3, 2)), ((3, 1),), ((3, 0),),
    )
    sequence = (0, 8, 3, 5, 1, 7, 2, 6, 4)

    def size_of(d, p):
        return (256, 256, 64)[p] if d in (0, 3) else (256, 192, 128)[p]

    def pick_of(table, k):
        return jnp.where(k == 0, table[0], jnp.where(k == 1, table[1], jnp.where(k == 2, table[2], table[3])))

    def my_rows(p, size):
        return pl.ds(pl.multiple_of(pick_of(begins[p], m), 64), size)

    def out(d, p, low):
        size = size_of(d, p)
        return remote(
            o_ref.at[pl.ds(d * ROWS + begins[p][d], size)],
            mixed.at[mine, pl.ds(begins[p][d], size)],
            o_send.at[d, p, low], o_recv.at[mine, p], 4 * group + d, low * 2 + core,
        )

    def local(d, p):
        size = size_of(d, p)
        return pltpu.make_async_copy(
            o_ref.at[pl.ds(d * ROWS + begins[p][d], size)],
            mixed.at[mine, pl.ds(begins[p][d], size)], lsem.at[p],
        )

    def give(tile):
        for d, p in parcels[tile]:
            for low in range(2):
                @pl.when((m != d) | (yl != low))
                def _():
                    out(d, p, low).start()

                @pl.when((m == d) & (yl == low))
                def _():
                    local(d, p).start()

    def landed(g, p, size):
        arrived(mixed.at[g, my_rows(p, size)], o_recv.at[g, p])

    def onward(d, low, p, size):
        g = head(d, low, core)
        ref = mixed.at[g, my_rows(p, size)]
        return remote(ref, ref, pass_send.at[d, p, low], o_recv.at[g, p], seq, mate)

    def sized(p, body):
        if p == 0:
            body(256)
        else:
            @pl.when(outer)
            def _():
                body(size_of(0, p))

            @pl.when((m == 1) | (m == 2))
            def _():
                body(size_of(1, p))

    def relay(p):
        def body(size):
            for d in range(4):
                for low in range(2):
                    @pl.when((m != d) | (yl != low))
                    def _():
                        landed(head(d, low, core), p, size)

                    @pl.when((m == d) & (yl == low))
                    def _():
                        ref = mixed.at[mine, my_rows(p, size)]
                        arrived(ref, lsem.at[p])

                    onward(d, low, p, size).start()

        sized(p, body)

    tiles = GROUP // TILE

    def turn_at(n):
        i = jnp.int32(sequence[-1])
        for k in range(tiles - 1):
            i = jnp.where(n == k, sequence[k], i)
        return i

    plain = group < 14

    @pl.when(plain)
    def _():
        score(jnp.int32(sequence[0]), 0)

    @pl.loop(0, tiles)
    def _(n):
        i = turn_at(n)
        rows = pl.ds(pl.multiple_of(i * TILE, TILE), TILE)
        first = group * GROUP + i * TILE

        for slot in range(2):
            @pl.when(plain & (n < tiles - 1) & (n % 2 == slot))
            def _():
                score(turn_at(n + 1), 1 - slot)
                weigh(i, slot)

        @pl.when(plain & (n == tiles - 1))
        def _():
            weigh(i, (tiles - 1) % 2)

        @pl.when((group >= 14) & (first < LONG))
        def _():
            score(i, 0)
            weigh(i, 0)

        @pl.when((group >= 14) & (first + TILE > LONG))
        def _():
            mixed_tile(i, rows, first)

        for tile in range(tiles):
            @pl.when(i == tile)
            def _():
                give(tile)

        for p in range(2):
            @pl.when(n == jnp.minimum(pick_of(turn_of[p], m) + 2, tiles - 1))
            def _():
                relay(p)

    partner = 1 - core

    def project_out(p):
        def body(size):
            for d in range(4):
                for low in range(2):
                    landed(head(d, low, partner), p, size)
            rows = my_rows(p, size)
            left = jnp.concatenate(
                [mixed[4 * order[k // 4] + k % 4, rows, :] for k in range(16)], axis=1
            )
            y_ref[rows, :] = jnp.dot(left, padded[...], preferred_element_type=jnp.float32)

        sized(p, body)

    cache_copy.wait()
    project_out(0)
    relay(2)
    project_out(1)
    project_out(2)

    @pl.loop(0, STEPS)
    def _(c):
        to_cross(c).wait_send()
        onward_x(c).wait_send()

    to_mate.wait_send()
    for copy in slabs:
        copy.wait_send()

    @pl.loop(0, 16)
    def _(n):
        c = n // 4
        s = n % 4
        spread(s, c).wait_send()
        spread_q(s, c).wait_send()

        @pl.when(xp == 0)
        def _():
            across(s, c).wait_send()

        @pl.when((xp == 1) & (z > 0))
        def _():
            passed(s, c).wait_send()

        @pl.when((z < 7) & needed(s, c))
        def _():
            ahead(s, c).wait_send()

    @pl.when(xp == 0)
    def _():
        sink_beside.wait_send()

        @pl.when(z < 7)
        def _():
            sink_ahead.wait_send()

    for d in range(4):
        for p in range(3):
            for low in range(2):
                @pl.when((m != d) | (yl != low))
                def _():
                    out(d, p, low).wait_send()

    for p in range(3):
        def body(size):
            for d in range(4):
                for low in range(2):
                    onward(d, low, p, size).wait_send()

        sized(p, body)


def shards(tokens, norm_gain, w_qkv, w_out, sink_logit, segment_ids, positions, padding_mask):
    bf16, f32 = jnp.bfloat16, jnp.float32
    spot = jnp.arange(PAD, dtype=jnp.int32)[None, :]
    info = jnp.where(
        spot == 0, positions[:, None], jnp.where(spot == 1, segment_ids[:, None], padding_mask[:, None])
    ).astype(f32)
    turns = THETA ** (-(np.arange(PAD) % 48) * 2.0 / HD) / (2.0 * np.pi)
    scale = 2.0 ** (np.floor(np.log2(turns)) - 7.0)
    high = np.floor(turns / scale) * scale
    freq = np.zeros((8, PAD), np.float32)
    freq[0] = high
    freq[1] = turns - high

    dma = pltpu.SemaphoreType.DMA
    y, cache = pl.pallas_call(
        whole_kernel,
        out_shape=(
            jax.ShapeDtypeStruct((ROWS, PART), f32),
            jax.ShapeDtypeStruct((2, ROWS, WIDTH), f32),
        ),
        in_specs=[ANY, VM, ANY, VM, VM, pl.BlockSpec(memory_space=pltpu.SMEM), ANY],
        out_specs=(VM, ANY),
        scratch_shapes=[
            pltpu.VMEM((4, ROWS, PART), bf16),
            pltpu.VMEM((4, 3, PART, WIDTH), bf16),
            pltpu.VMEM((ROWS, 3 * WIDTH), f32),
            pltpu.VMEM((ROWS, 1), f32),
            pltpu.VMEM((4, ROWS, PAD), f32),
            pltpu.VMEM((4, ROWS, PAD), bf16),
            pltpu.VMEM((4, ROWS, 2 * PAD), bf16),
            pltpu.VMEM((2, ROWS, WIDTH), f32),
            pltpu.VMEM((GROUP, PAD), bf16),
            pltpu.VMEM((SPAN, 2 * PAD), bf16),
            pltpu.VMEM((TILE, WINDOW), f32),
            pltpu.VMEM((TILE, WINDOW), f32),
            pltpu.VMEM((2, TILE, 1), f32),
            pltpu.VMEM((GROUP, PAD), bf16),
            pltpu.VMEM((16, ROWS, PAD), bf16),
            pltpu.VMEM((3, WIDTH, PART), bf16),
            pltpu.VMEM((WIDTH, PART), bf16),
            pltpu.VMEM((16 * PAD, PART), bf16),
            dma((5,)), dma, dma((9,)), dma((9,)), dma((3,)), dma((3,)),
            dma((4, 4)), dma((4, 4)), dma((4, 4)), dma((4, 4)),
            dma((4, 4)), dma((4, 4)), dma((4, 4)), dma((4, 4)), dma((2,)), dma,
            dma((4, 3, 2)), dma((16, 3)), dma((4, 3, 2)), dma((3,)), dma,
        ],
        compiler_params=pltpu.CompilerParams(
            collective_id=0, has_side_effects=True, vmem_limit_bytes=62 * 1024 * 1024
        ),
        name="whole",
    )(
        tokens, norm_gain.reshape(1, MODEL), jnp.transpose(w_qkv, (1, 0, 2)), info,
        jnp.asarray(freq), sink_logit, w_out,
    )
    return (y.astype(bf16), cache.astype(bf16))


def solution(mesh):
    return jax.shard_map(
        shards,
        mesh=mesh,
        in_specs=(
            P("seq", "tp"),
            P(),
            P(None, None, "tp"),
            P("tp", None),
            P("tp"),
            P("seq"),
            P("seq"),
            P("seq"),
        ),
        out_specs=(P("seq", "tp"), P(None, "seq", "tp")),
        check_vma=False,
    )
```

```python
import math

import jax
import jax.numpy as jnp
import numpy as np
from jax import lax
from jax.experimental import pallas as pl
from jax.experimental.pallas import tpu as pltpu
from jax.sharding import PartitionSpec as P

WINDOW = 4096
SINKS = 4
EPS = 1e-05
THETA = 10000.0
LONG = 32832

ROWS = 576
MODEL = 3072
PART = 768
WIDTH = 384
HD = 96
PAD = 128
GROUP = 2304
TILE = 256
CHUNK = 144
STEPS = 4
PREV1 = GROUP
OWN = 2 * GROUP
SINK_AT = 3 * GROUP
SPAN = 3 * GROUP + 16
FAR = 512
NEG = -1e30
MESH = pl.DeviceIdType.MESH
ANY = pl.BlockSpec(memory_space=pl.ANY)
VM = pl.BlockSpec(memory_space=pltpu.VMEM)


def place():
    seq = lax.axis_index("seq")
    tp = lax.axis_index("tp")
    return seq, tp, tp // 2, tp % 2


def remote(src, dst, send, recv, seq, tp):
    return pltpu.make_async_remote_copy(
        src_ref=src,
        dst_ref=dst,
        send_sem=send,
        recv_sem=recv,
        device_id=(seq, tp),
        device_id_type=MESH,
    )


def arrived(ref, sem):
    pltpu.make_async_copy(ref, ref, sem).wait()


def greet(seq, tp):
    pl.semaphore_signal(
        pltpu.get_barrier_semaphore(), inc=1, device_id=(seq, tp), device_id_type=MESH
    )


def lanes(rows):
    return lax.broadcasted_iota(jnp.int32, (rows, PAD), 1)


def dot_t(a, b):
    return lax.dot_general(a, b, (((1,), (1,)), ((), ())), preferred_element_type=jnp.float32)


def whole_kernel(
    x_ref, gain_ref, w_ref, info_ref, freq_ref, logit_ref, wo_ref,
    y_ref, cache_ref,
    held, weights, acc, square, mark_s, q_s, kv_s, qo, kv, scores_a, scores_b, peaks, o_ref, mixed, wg, slab, padded,
    wsem, xsem, send, recv, wsend, wrecv, a_send, a_recv, b_send, b_recv,
    x_send, z_send, one_recv, two_recv, s_send, s_recv, o_send, o_recv, pass_send, lsem,
):
    scores = (scores_a, scores_b)
    seq, tp, yl, core = place()
    group = seq // 4
    m = seq % 4
    z = seq // 8
    xp = group % 2
    xb = m // 2
    hy = m % 2
    mate = yl * 2 + 1 - core
    cross = (1 - yl) * 2 + core
    far = (1 - yl) * 2 + 1 - core
    flipped = seq + 1 - 2 * hy
    beside = 4 * (group + 1 - 2 * xp) + (1 - xb) * 2 + hy
    order = (tp, mate, cross, far)

    def wide(t):
        return pl.ds(pl.multiple_of(t * PART, PART), PART)

    own = pltpu.make_async_copy(x_ref, held.at[0], xsem)
    own.start()

    def weight_copy(k):
        return pltpu.make_async_copy(w_ref.at[:, wide(order[k]), :], weights.at[k], wsem.at[k])

    for k in range(4):
        weight_copy(k).start()
    own_slab = pltpu.make_async_copy(wo_ref.at[:, wide(tp)], slab, wsem.at[4])
    own_slab.start()

    greet(seq, mate)
    greet(flipped, far)
    greet(beside, tp)
    for d in range(4):
        for low in range(2):
            @pl.when((m != d) | (yl != low))
            def _():
                greet(4 * group + d, low * 2 + core)

    @pl.when(z > 0)
    def _():
        greet(seq - 8, tp)

    @pl.when(z < 7)
    def _():
        greet(seq + 8, tp)

    pl.semaphore_wait(
        pltpu.get_barrier_semaphore(), 10 + jnp.where(z > 0, 1, 0) + jnp.where(z < 7, 1, 0)
    )

    def part(c):
        return pl.ds(pl.multiple_of(c * CHUNK, CHUNK), CHUNK)

    def to_cross(c):
        return remote(x_ref.at[part(c)], held.at[2, part(c)], send.at[c], recv.at[c], seq, cross)

    def onward_x(c):
        return remote(
            held.at[2, part(c)], held.at[3, part(c)], send.at[4 + c], recv.at[4 + c], seq, mate
        )

    @pl.loop(0, STEPS)
    def _(c):
        to_cross(c).start()

    to_mate = remote(x_ref, held.at[1], send.at[8], recv.at[8], seq, mate)
    to_mate.start()
    slabs = [
        remote(wo_ref.at[:, wide(t2)], wg.at[n], wsend.at[n], wrecv.at[n], s2, t2)
        for n, (s2, t2) in enumerate(((seq, mate), (seq, cross), (flipped, far)))
    ]

    def blank(start, size):
        mark = lax.broadcasted_iota(jnp.int32, (16, 2 * PAD), 1)
        row = jnp.where(mark == 102, 1.0, 0.0).astype(jnp.bfloat16)

        @pl.loop(0, size // 16)
        def _(n):
            kv[pl.ds(pl.multiple_of(start + n * 16, 16), 16), :] = row

    @pl.when(group == 0)
    def _():
        blank(PREV1, GROUP)
        blank(SINK_AT, 16)

    @pl.when(group < 2)
    def _():
        blank(FAR, GROUP - FAR)

    lane_row = lanes(1)
    sinks = []
    for h in range(4):
        logit = jnp.full((1, PAD), logit_ref[h], jnp.float32) * (1.0 / math.log(2.0))
        high = logit.astype(jnp.bfloat16).astype(jnp.float32)
        sinks.append(jnp.where(lane_row == 98, high, jnp.where(lane_row == 99, logit - high, 0.0)))

    def tables(c):
        rows = part(c)
        lane = lanes(CHUNK)
        info = info_ref[rows, :]
        pos = info[:, 0:1]
        seg = info[:, 1:2]
        lost = 1.0 - info[:, 2:3]
        first = jnp.where(pos < SINKS, 1.0, 0.0)
        mark_s[0, rows, :] = jnp.where(
            lane == 96, seg,
            jnp.where(
                lane == 97, 1.0,
                jnp.where((lane == 98) | (lane == 99), first, jnp.where(lane == 100, lost, 0.0)),
            ),
        )
        mark_s[1, rows, :] = jnp.where(lane == 101, seg, jnp.where(lane == 102, NEG, 0.0))
        turns = pos * freq_ref[0:1, :]
        turns = (turns - jnp.round(turns)) + pos * freq_ref[1:2, :]
        angle = (turns - jnp.round(turns)) * (2.0 * math.pi)
        sine = jnp.sin(angle)
        mark_s[2, rows, :] = jnp.cos(angle)
        mark_s[3, rows, :] = jnp.where(lane < 48, -sine, sine)

    def block(k, c):
        rows = part(c)
        x = held[k, rows, :].astype(jnp.float32)
        sums = jnp.sum(x * x, axis=-1, keepdims=True)
        y = (x * gain_ref[:, wide(order[k])]).astype(jnp.bfloat16)
        if k == 0:
            square[rows, :] = sums
        else:
            square[rows, :] += sums
        for j in range(3):
            cols = pl.ds(j * WIDTH, WIDTH)
            term = jnp.dot(y, weights[k, j], preferred_element_type=jnp.float32)
            if k == 0:
                acc[rows, cols] = term
            else:
                acc[rows, cols] += term

    def close(c):
        rows = part(c)
        lane = lanes(CHUNK)
        factor = lax.rsqrt(square[rows, :] / MODEL + EPS)
        info = info_ref[rows, :]
        valid = info[:, 2:3]
        kmark = mark_s[0, rows, :]
        qmark = mark_s[1, rows, :]
        cosine = mark_s[2, rows, :]
        sine = mark_s[3, rows, :]

        def heads(j):
            b = [acc[rows, pl.ds(j * WIDTH + n * PAD, PAD)] * factor for n in range(3)]
            return b, [
                b[0],
                jnp.where(lane < 32, pltpu.roll(b[0], 32, 1), pltpu.roll(b[1], 32, 1)),
                jnp.where(lane < 64, pltpu.roll(b[1], 64, 1), pltpu.roll(b[2], 64, 1)),
                pltpu.roll(b[2], 96, 1),
            ]

        def turn(u):
            other = jnp.where(lane < 48, pltpu.roll(u, 80, 1), pltpu.roll(u, 48, 1))
            return jnp.where(lane < HD, u * cosine + other * sine, 0.0)

        for h, u in enumerate(heads(0)[1]):
            full = turn(u) * (HD ** -0.5 / math.log(2.0)) + qmark + sinks[h]
            q_s[h, rows, :] = full.astype(jnp.bfloat16)
        keys = []
        for h, u in enumerate(heads(1)[1]):
            k = turn(u)
            keys.append(k)
            kv_s[h, rows, 0:PAD] = (k + kmark).astype(jnp.bfloat16)
        k1, k2, k3 = (pltpu.roll(keys[1], 96, 1), pltpu.roll(keys[2], 64, 1), pltpu.roll(keys[3], 32, 1))
        joined = (
            jnp.where(lane < 96, keys[0], k1),
            jnp.where(lane < 64, k1, k2),
            jnp.where(lane < 32, k2, k3),
        )
        plain, values = heads(2)
        for n in range(3):
            cols = pl.ds(n * PAD, PAD)
            cache_ref[0, rows, cols] = joined[n] * valid
            cache_ref[1, rows, cols] = plain[n] * valid
        for h, u in enumerate(values):
            v = jnp.where(lane < HD, u, jnp.where(lane == HD, 1.0, 0.0))
            kv_s[h, rows, PAD:] = v.astype(jnp.bfloat16)

    def piece(base, s, c):
        return pl.ds(pl.multiple_of(base + s * ROWS + c * CHUNK, 16), CHUNK)

    def head_of(d):
        b = d // 2
        return (b + xp - 2 * xp * b) * 2 + d % 2

    def spread(d, c):
        return remote(
            kv_s.at[head_of(d), part(c)], kv.at[piece(OWN, m, c)],
            a_send.at[d, c], a_recv.at[m, c], 4 * group + d, cross,
        )

    def spread_q(d, c):
        return remote(
            q_s.at[head_of(d), part(c)], qo.at[piece(0, m, c)],
            b_send.at[d, c], b_recv.at[m, c], 4 * group + d, cross,
        )

    def across(s, c):
        return remote(
            kv.at[piece(OWN, s, c)], kv.at[piece(PREV1, s, c)],
            x_send.at[s, c], one_recv.at[s, c], beside, tp,
        )

    def passed(s, c):
        return remote(
            kv.at[piece(0, s, c)], kv.at[piece(PREV1, s, c)],
            x_send.at[s, c], one_recv.at[s, c], beside, tp,
        )

    def ahead(s, c):
        return remote(
            kv.at[piece(OWN, s, c)], kv.at[piece(0, s, c)],
            z_send.at[s, c], two_recv.at[s, c], seq + 8, tp,
        )

    sink_rows = kv.at[pl.ds(SINK_AT, 16)]
    sink_from = kv.at[pl.ds(pl.multiple_of(jnp.where(z == 0, OWN, SINK_AT), 16), 16)]
    sink_beside = remote(sink_from, sink_rows, s_send.at[0], s_recv, beside, tp)
    sink_ahead = remote(sink_from, sink_rows, s_send.at[1], s_recv, seq + 8, tp)

    def needed(s, c):
        return (xp == 1) | (s > 0) | (c == STEPS - 1)

    def serve(n):
        c = n // 4
        s = n % 4

        @pl.when(n < 16)
        def _():
            arrived(kv.at[piece(OWN, s, c)], a_recv.at[s, c])

            @pl.when(xp == 0)
            def _():
                across(s, c).start()

            @pl.when((z < 7) & needed(s, c))
            def _():
                ahead(s, c).start()

        @pl.when((n == z) & (xp == 0))
        def _():
            @pl.when(z > 0)
            def _():
                arrived(sink_rows, s_recv)

            sink_beside.start()

            @pl.when(z < 7)
            def _():
                sink_ahead.start()

        @pl.when((n >= 4) & (xp == 1) & (z > 0))
        def _():
            arrived(kv.at[piece(0, s, c - 1)], two_recv.at[s, c - 1])
            passed(s, c - 1).start()

    @pl.loop(0, STEPS)
    def _(c):
        tables(c)

    own.wait()
    weight_copy(0).wait()

    @pl.loop(0, STEPS)
    def _(c):
        block(0, c)

    to_mate.wait_recv()
    weight_copy(1).wait()

    @pl.loop(0, STEPS)
    def _(c):
        block(1, c)

    weight_copy(2).wait()
    weight_copy(3).wait()

    @pl.loop(0, STEPS + 1)
    def _(c):
        @pl.when(c < STEPS)
        def _():
            to_cross(c).wait_recv()
            onward_x(c).start()
            block(2, c)

        @pl.when(c > 0)
        def _():
            onward_x(c - 1).wait_recv()
            block(3, c - 1)
            close(c - 1)
            for d in range(4):
                spread(d, c - 1).start()

        @pl.when(c > 2)
        def _():
            @pl.loop(0, 4)
            def _(n):
                serve((c - 3) * 4 + n)

    @pl.loop(0, STEPS)
    def _(c):
        for d in range(4):
            spread_q(d, c).start()

    for copy in slabs:
        copy.start()

    @pl.loop(8, 20)
    def _(n):
        serve(n)

    own_slab.wait()
    for n in range(16):
        padded[pl.ds(n * PAD + HD, PAD - HD), :] = jnp.zeros((PAD - HD, PART), jnp.bfloat16)
    for n in range(4):
        padded[pl.ds(n * PAD, HD), :] = slab[pl.ds(n * HD, HD), :]

    @pl.loop(0, 16)
    def _(n):
        c = n // 4
        s = n % 4
        arrived(qo.at[piece(0, s, c)], b_recv.at[s, c])

        @pl.when((xp == 0) & (z > 0) & needed(s, c))
        def _():
            arrived(kv.at[piece(0, s, c)], two_recv.at[s, c])

        @pl.when((xp == 1) | (z > 0))
        def _():
            arrived(kv.at[piece(PREV1, s, c)], one_recv.at[s, c])

    @pl.when(xp == 1)
    def _():
        arrived(sink_rows, s_recv)

    def key(start, size):
        return kv[pl.ds(pl.multiple_of(start, TILE), size), 0:PAD]

    def val(start, size):
        return kv[pl.ds(pl.multiple_of(start, TILE), size), PAD:]

    down = lax.broadcasted_iota(jnp.int32, (TILE, TILE), 0)
    right = lax.broadcasted_iota(jnp.int32, (TILE, TILE), 1)
    lower = right <= down
    sink_k = kv[pl.ds(SINK_AT, 16), 0:PAD]
    sink_v = kv[pl.ds(SINK_AT, 16), PAD:]
    small_down = lax.broadcasted_iota(jnp.int32, (TILE, 16), 0)
    small_right = lax.broadcasted_iota(jnp.int32, (TILE, 16), 1)

    def finish(rows, acc):
        lane = lanes(TILE)
        out = acc * (1.0 / acc[:, HD:HD + 1])
        o_ref[rows, :] = jnp.where(lane < HD, out, 0.0).astype(jnp.bfloat16)

    def sink_part(q, first):
        distance = first + small_down - small_right
        seen = (small_right < SINKS) & (distance >= WINDOW)
        return seen, jnp.where(seen, dot_t(q, sink_k), NEG)

    def score(i, slot):
        rows = pl.ds(pl.multiple_of(i * TILE, TILE), TILE)
        first = group * GROUP + i * TILE
        keep = scores[slot]
        q = qo[rows, :]
        near = OWN + i * TILE
        outer = FAR + i * TILE
        s = jnp.where(lower, dot_t(q, key(near, TILE)), dot_t(q, key(outer, TILE)))
        keep[:, 0:TILE] = s
        top = jnp.maximum(s[:, :PAD], s[:, PAD:])
        sink_s = sink_part(q, first)[1]
        for c in range(5):
            s = dot_t(q, key(outer + TILE + c * 768, 768))
            keep[:, pl.ds(TILE + c * 768, 768)] = s
            for n in range(6):
                top = jnp.maximum(top, s[:, n * PAD:(n + 1) * PAD])
        peaks[slot, :, :] = jnp.maximum(
            jnp.max(top, axis=-1, keepdims=True), jnp.max(sink_s, axis=-1, keepdims=True)
        )

    def weigh(i, slot):
        rows = pl.ds(pl.multiple_of(i * TILE, TILE), TILE)
        first = group * GROUP + i * TILE
        keep = scores[slot]
        q = qo[rows, :]
        near = OWN + i * TILE
        outer = FAR + i * TILE
        peak = peaks[slot, :, :]
        seen, sink_s = sink_part(q, first)
        w = jnp.where(seen, jnp.exp2(sink_s - peak), 0.0).astype(jnp.bfloat16)
        acc = jnp.dot(w, sink_v, preferred_element_type=jnp.float32)
        w = jnp.exp2(keep[:, 0:TILE] - peak)
        acc += jnp.dot(
            jnp.where(lower, w, 0.0).astype(jnp.bfloat16), val(near, TILE), preferred_element_type=jnp.float32
        )
        acc += jnp.dot(
            jnp.where(lower, 0.0, w).astype(jnp.bfloat16), val(outer, TILE), preferred_element_type=jnp.float32
        )
        for c in range(5):
            w = jnp.exp2(keep[:, pl.ds(TILE + c * 768, 768)] - peak).astype(jnp.bfloat16)
            acc += jnp.dot(w, val(outer + TILE + c * 768, 768), preferred_element_type=jnp.float32)
        finish(rows, acc)

    def mixed_tile(i, rows, first):
        q = qo[rows, :]
        lane = lanes(TILE)
        qf = q.astype(jnp.float32)
        mine = qf[:, 101:102]
        pick = jnp.where(lane == 96, -1.0, jnp.where(lane == 97, mine, 0.0)).astype(jnp.bfloat16)
        lost = jnp.where(lane == 100, 1.0, 0.0).astype(jnp.bfloat16)
        distance = first + small_down - small_right
        seen = (small_right < SINKS) & (distance >= WINDOW) & (dot_t(pick, sink_k) == 0.0)
        sink_s = jnp.where(seen, dot_t(q, sink_k), NEG)
        peak = jnp.max(sink_s, axis=-1, keepdims=True)
        w = jnp.where(seen, jnp.exp2(sink_s - peak), 0.0).astype(jnp.bfloat16)
        acc = jnp.dot(w, sink_v, preferred_element_type=jnp.float32)
        def step(n, carry):
            peak, acc = carry
            start = FAR + i * TILE + n * TILE
            k = key(start, TILE)
            gap = (16 - n) * TILE + down - right
            bad = dot_t(lost, k)
            seen = (gap >= 0) & (gap < WINDOW) & (dot_t(pick, k) == 0.0) & ((bad < 0.5) | (gap == 0))
            s = jnp.where(seen, dot_t(q, k), NEG)
            now = jnp.maximum(peak, jnp.max(s, axis=-1, keepdims=True))
            w = jnp.where(seen, jnp.exp2(s - now), 0.0).astype(jnp.bfloat16)
            acc = acc * jnp.exp2(peak - now) + jnp.dot(w, val(start, TILE), preferred_element_type=jnp.float32)
            return now, acc

        peak, acc = lax.fori_loop(15, 17, step, (peak, acc))
        out = acc * (1.0 / acc[:, HD:HD + 1])
        out = jnp.where(lane < HD, out, 0.0).astype(jnp.bfloat16)
        short = first + lax.broadcasted_iota(jnp.int32, (TILE, PAD), 0) >= LONG
        o_ref[rows, :] = jnp.where(short, out, o_ref[rows, :])

    def head(member, low, who):
        b = member // 2
        return 4 * ((1 - low) * 2 + who) + (b + xp - 2 * xp * b) * 2 + member % 2

    mine = head(m, yl, core)
    outer = (m == 0) | (m == 3)
    begins = ((0, 192, 128, 320), (256, 0, 384, 64), (512, 448, 0, 0))
    turn_of = ((0, 2, 3, 1), (4, 6, 7, 5))
    parcels = (
        ((0, 0),), ((0, 1),), ((0, 2), (1, 1)), ((1, 0),), ((1, 2), (2, 2)),
        ((2, 0),), ((2, 1), (3, 2)), ((3, 1),), ((3, 0),),
    )
    sequence = (0, 8, 3, 5, 1, 7, 2, 6, 4)

    def size_of(d, p):
        return (256, 256, 64)[p] if d in (0, 3) else (256, 192, 128)[p]

    def pick_of(table, k):
        return jnp.where(k == 0, table[0], jnp.where(k == 1, table[1], jnp.where(k == 2, table[2], table[3])))

    def my_rows(p, size):
        return pl.ds(pl.multiple_of(pick_of(begins[p], m), 64), size)

    def out(d, p, low):
        size = size_of(d, p)
        return remote(
            o_ref.at[pl.ds(d * ROWS + begins[p][d], size)],
            mixed.at[mine, pl.ds(begins[p][d], size)],
            o_send.at[d, p, low], o_recv.at[mine, p], 4 * group + d, low * 2 + core,
        )

    def local(d, p):
        size = size_of(d, p)
        return pltpu.make_async_copy(
            o_ref.at[pl.ds(d * ROWS + begins[p][d], size)],
            mixed.at[mine, pl.ds(begins[p][d], size)], lsem.at[p],
        )

    def give(tile):
        for d, p in parcels[tile]:
            for low in range(2):
                @pl.when((m != d) | (yl != low))
                def _():
                    out(d, p, low).start()

                @pl.when((m == d) & (yl == low))
                def _():
                    local(d, p).start()

    def landed(g, p, size):
        arrived(mixed.at[g, my_rows(p, size)], o_recv.at[g, p])

    def onward(d, low, p, size):
        g = head(d, low, core)
        ref = mixed.at[g, my_rows(p, size)]
        return remote(ref, ref, pass_send.at[d, p, low], o_recv.at[g, p], seq, mate)

    def sized(p, body):
        if p == 0:
            body(256)
        else:
            @pl.when(outer)
            def _():
                body(size_of(0, p))

            @pl.when((m == 1) | (m == 2))
            def _():
                body(size_of(1, p))

    def relay(p):
        def body(size):
            for d in range(4):
                for low in range(2):
                    @pl.when((m != d) | (yl != low))
                    def _():
                        landed(head(d, low, core), p, size)

                    @pl.when((m == d) & (yl == low))
                    def _():
                        ref = mixed.at[mine, my_rows(p, size)]
                        arrived(ref, lsem.at[p])

                    onward(d, low, p, size).start()

        sized(p, body)

    tiles = GROUP // TILE

    def turn_at(n):
        i = jnp.int32(sequence[-1])
        for k in range(tiles - 1):
            i = jnp.where(n == k, sequence[k], i)
        return i

    plain = group < 14

    @pl.when(plain)
    def _():
        score(jnp.int32(sequence[0]), 0)

    @pl.loop(0, tiles)
    def _(n):
        i = turn_at(n)
        rows = pl.ds(pl.multiple_of(i * TILE, TILE), TILE)
        first = group * GROUP + i * TILE

        for slot in range(2):
            @pl.when(plain & (n < tiles - 1) & (n % 2 == slot))
            def _():
                score(turn_at(n + 1), 1 - slot)
                weigh(i, slot)

        @pl.when(plain & (n == tiles - 1))
        def _():
            weigh(i, (tiles - 1) % 2)

        @pl.when((group >= 14) & (first < LONG))
        def _():
            score(i, 0)
            weigh(i, 0)

        @pl.when((group >= 14) & (first + TILE > LONG))
        def _():
            mixed_tile(i, rows, first)

        for tile in range(tiles):
            @pl.when(i == tile)
            def _():
                give(tile)

        @pl.when(n == tiles - 2)
        def _():
            for copy in slabs:
                copy.wait_recv()
            for k in range(12):
                padded[pl.ds((k + 4) * PAD, HD), :] = wg[k // 4, pl.ds(k % 4 * HD, HD), :]

        for p in range(2):
            @pl.when(n == jnp.minimum(pick_of(turn_of[p], m) + 2, tiles - 1))
            def _():
                relay(p)

    partner = 1 - core

    def project_out(p):
        def body(size):
            for d in range(4):
                for low in range(2):
                    landed(head(d, low, partner), p, size)
            rows = my_rows(p, size)
            left = jnp.concatenate(
                [mixed[4 * order[k // 4] + k % 4, rows, :] for k in range(16)], axis=1
            )
            y_ref[rows, :] = jnp.dot(left, padded[...], preferred_element_type=jnp.float32)

        sized(p, body)

    project_out(0)
    relay(2)
    project_out(1)
    project_out(2)

    @pl.loop(0, STEPS)
    def _(c):
        to_cross(c).wait_send()
        onward_x(c).wait_send()

    to_mate.wait_send()
    for copy in slabs:
        copy.wait_send()

    @pl.loop(0, 16)
    def _(n):
        c = n // 4
        s = n % 4
        spread(s, c).wait_send()
        spread_q(s, c).wait_send()

        @pl.when(xp == 0)
        def _():
            across(s, c).wait_send()

        @pl.when((xp == 1) & (z > 0))
        def _():
            passed(s, c).wait_send()

        @pl.when((z < 7) & needed(s, c))
        def _():
            ahead(s, c).wait_send()

    @pl.when(xp == 0)
    def _():
        sink_beside.wait_send()

        @pl.when(z < 7)
        def _():
            sink_ahead.wait_send()

    for d in range(4):
        for p in range(3):
            for low in range(2):
                @pl.when((m != d) | (yl != low))
                def _():
                    out(d, p, low).wait_send()

    for p in range(3):
        def body(size):
            for d in range(4):
                for low in range(2):
                    onward(d, low, p, size).wait_send()

        sized(p, body)


def shards(tokens, norm_gain, w_qkv, w_out, sink_logit, segment_ids, positions, padding_mask):
    bf16, f32 = jnp.bfloat16, jnp.float32
    spot = jnp.arange(PAD, dtype=jnp.int32)[None, :]
    info = jnp.where(
        spot == 0, positions[:, None], jnp.where(spot == 1, segment_ids[:, None], padding_mask[:, None])
    ).astype(f32)
    turns = THETA ** (-(np.arange(PAD) % 48) * 2.0 / HD) / (2.0 * np.pi)
    scale = 2.0 ** (np.floor(np.log2(turns)) - 7.0)
    high = np.floor(turns / scale) * scale
    freq = np.zeros((8, PAD), np.float32)
    freq[0] = high
    freq[1] = turns - high

    dma = pltpu.SemaphoreType.DMA
    y, cache = pl.pallas_call(
        whole_kernel,
        out_shape=(
            jax.ShapeDtypeStruct((ROWS, PART), f32),
            jax.ShapeDtypeStruct((2, ROWS, WIDTH), f32),
        ),
        in_specs=[ANY, VM, ANY, VM, VM, pl.BlockSpec(memory_space=pltpu.SMEM), ANY],
        out_specs=(VM, VM),
        scratch_shapes=[
            pltpu.VMEM((4, ROWS, PART), bf16),
            pltpu.VMEM((4, 3, PART, WIDTH), bf16),
            pltpu.VMEM((ROWS, 3 * WIDTH), f32),
            pltpu.VMEM((ROWS, 1), f32),
            pltpu.VMEM((4, ROWS, PAD), f32),
            pltpu.VMEM((4, ROWS, PAD), bf16),
            pltpu.VMEM((4, ROWS, 2 * PAD), bf16),
            pltpu.VMEM((GROUP, PAD), bf16),
            pltpu.VMEM((SPAN, 2 * PAD), bf16),
            pltpu.VMEM((TILE, WINDOW), f32),
            pltpu.VMEM((TILE, WINDOW), f32),
            pltpu.VMEM((2, TILE, 1), f32),
            pltpu.VMEM((GROUP, PAD), bf16),
            pltpu.VMEM((16, ROWS, PAD), bf16),
            pltpu.VMEM((3, WIDTH, PART), bf16),
            pltpu.VMEM((WIDTH, PART), bf16),
            pltpu.VMEM((16 * PAD, PART), bf16),
            dma((5,)), dma, dma((9,)), dma((9,)), dma((3,)), dma((3,)),
            dma((4, 4)), dma((4, 4)), dma((4, 4)), dma((4, 4)),
            dma((4, 4)), dma((4, 4)), dma((4, 4)), dma((4, 4)), dma((2,)), dma,
            dma((4, 3, 2)), dma((16, 3)), dma((4, 3, 2)), dma((3,)),
        ],
        compiler_params=pltpu.CompilerParams(
            collective_id=0, has_side_effects=True, vmem_limit_bytes=62 * 1024 * 1024
        ),
        name="whole",
    )(
        tokens, norm_gain.reshape(1, MODEL), jnp.transpose(w_qkv, (1, 0, 2)), info,
        jnp.asarray(freq), sink_logit, w_out,
    )
    return (y.astype(bf16), cache.astype(bf16))


def solution(mesh):
    return jax.shard_map(
        shards,
        mesh=mesh,
        in_specs=(
            P("seq", "tp"),
            P(),
            P(None, None, "tp"),
            P("tp", None),
            P("tp"),
            P("seq"),
            P("seq"),
            P("seq"),
        ),
        out_specs=(P("seq", "tp"), P(None, "seq", "tp")),
        check_vma=False,
    )
```
